128 devices in a mesh: attn: 4 (over x), expert: 32 (over y, z, core).
Axes of the slice: x: 4, y: 4, z: 4, core: 2. Of those that a mesh axis runs over, the one named last changes fastest.
Arguments:
- tokens: bfloat16 [2, 1024, 7168], P(None, ('attn', 'expert')), may hold values from -6 to 6
- routes: int32 [2, 1024, 8], P(None, ('attn', 'expert')), may hold values from 0 to 47, all different within a row; in each aligned block of 8 rows (0 to 7, 8 to 15, ..., all dimensions but the last counted through in order) at most 2 rows name the same one
- route_weights: float32 [2, 1024, 8], P(None, ('attn', 'expert')), may hold values from 0.2 to 1
- slot_expert: int32 [64], replicated, may hold values from 0 to 47, as said below
- w_gate: bfloat16 [64, 7168, 1024], P('expert', None, 'attn'), as said below
- w_up: bfloat16 [64, 7168, 1024], P('expert', None, 'attn'), as said below
- w_down: bfloat16 [64, 1024, 7168], P('expert', 'attn'), as said below
Outputs:
- combined: bfloat16 [2, 1024, 7168], P(None, ('attn', 'expert'))
The draws below stay inside these ranges and needn't reach their ends.
Inputs may be any that keep to these rules, and one draw needn't show every extreme that they name: `routes`: in each micro-step at most 2 of one device's 8 rows choose the same expert, and some expert reaches 2. `slot_expert`: every expert of the window is held by at least one slot; some are held by several. `w_gate`: slots that hold the same expert hold identical gate projections. `w_up`: slots that hold the same expert hold identical up projections. `w_down`: slots that hold the same expert hold identical down projections.
All inputs are finite; a program needn't handle non-finite values.
Results may differ from the reference program's by a relative error of at most 0.0064.
Values may be sent and summed in bfloat16 or wider, within the bound.
No kernel may reach another device: no remote copies, remote signals or barrier semaphores. Data moves between devices by JAX's collectives and lax.ppermute only.
A program may use at most 128 MiB of HBM per device.

```python
import math
import jax
import jax.numpy as jnp
import numpy as np
from jax import lax

D = 7168
TOP = 8
HID = 1024
TOK_DEV = 8
MICRO = 2
HGROUPS = 4
QUART = 256
SLOTS = 64
EXPERTS = 48
TOKENS = 1024
CAP = 2
N_ATTN = 4
N_EXPERT = 32


def slot_table(key):
    base_key = jax.random.fold_in(key, 101)
    first_key, second_key, third_key = jax.random.split(base_key, 3)
    base = jax.random.permutation(first_key, EXPERTS).astype(jnp.int32)
    extra = jax.random.randint(second_key, (SLOTS - EXPERTS,), 0, EXPERTS).astype(jnp.int32)
    table = jnp.concatenate([base, extra])
    return jax.random.permutation(third_key, table).astype(jnp.int32)


def draw_slot_expert(key, part):
    return slot_table(key)


def draw_w_gate(key, part):
    salted = jax.random.fold_in(key, 11)
    values = jax.random.normal(salted, (EXPERTS, D, HID), jnp.float32)
    values = values * D ** (-0.5)
    return values[slot_table(key)].astype(jnp.bfloat16)


def draw_w_up(key, part):
    salted = jax.random.fold_in(key, 12)
    values = jax.random.normal(salted, (EXPERTS, D, HID), jnp.float32)
    values = values * D ** (-0.5)
    return values[slot_table(key)].astype(jnp.bfloat16)


def draw_w_down(key, part):
    salted = jax.random.fold_in(key, 13)
    values = jax.random.normal(salted, (EXPERTS, HID, D), jnp.float32)
    values = values * HID ** (-0.5)
    return values[slot_table(key)].astype(jnp.bfloat16)


def shard_levels(stream_key, extent, shards, least, top_value):
    loudness, own = 1.0, jax.random.fold_in(stream_key, 6)
    for position, shards_of in shards:
        heights = jnp.exp(jax.random.uniform(jax.random.fold_in(own, position), (shards_of,), jnp.float32, least / len(shards), top_value / len(shards)))
        loudness = loudness * jnp.repeat(heights, extent[position] // shards_of).reshape([-1 if axis == position else 1 for axis in range(len(extent))])
    return loudness


def routed_block(own_key, own, number, rows, count, top, reach, lean):
    ranking = jax.random.permutation(own_key, count)
    heavy_load, common = load_shares(count, rows * top, reach, lean, True), load_shares(count, rows * top, reach, lean, False)
    places = jnp.arange(count)

    def named(lengths, turn):
        used = int((lengths > 0).sum())
        fixed = max(1, used // 4)
        passed = fixed + (places - fixed + turn * (used - fixed)) % max(1, count - fixed)
        return jnp.zeros((count,), jnp.int32).at[ranking[jnp.where(places < fixed, places, passed)]].set(jnp.asarray(lengths, jnp.int32))

    lengths = jnp.where(number % 4 == 0, named(heavy_load, number // 4), named(common, number - number // 4 - 1))
    mixed = jax.random.permutation(jax.random.fold_in(own, 3), count)
    donor, sink = mixed[0:count // 2 * 2:2], mixed[1:count // 2 * 2:2]
    room = jnp.minimum(lengths[donor] - 1, reach - lengths[sink]) // 2
    room = jnp.where((donor == ranking[0]) | (sink == ranking[0]) | (lengths[sink] == 0), 0, jnp.maximum(room, 0))
    passed = jax.random.randint(jax.random.fold_in(own, 4), (count // 2,), 0, 1 << 20) % (room + 1)
    lengths = lengths.at[donor].add(-passed).at[sink].add(passed)
    items = jnp.searchsorted(jnp.cumsum(lengths), jnp.arange(rows * top), side="right").astype(jnp.int32)
    listing = items.reshape(top, rows).T
    listing = listing[jax.random.permutation(jax.random.fold_in(own, 1), rows)]
    turn = jax.random.randint(jax.random.fold_in(own, 2), (rows, 1), 0, top)
    return jnp.take_along_axis(listing, (jnp.arange(top)[None, :] + turn) % top, axis=1)


def load_shares(number_of, total, bound, skew, full):
    portions = [(1 << 20) // math.isqrt(standing ** skew) + 1 for standing in range(1, number_of + 1)]
    largest = bound if full else min(bound, max(-(-total // number_of), total * portions[0] // sum(portions)))
    least = 1 if total - largest >= number_of - 1 else 0
    given, surplus = [largest] + [least] * (number_of - 1), total - largest - least * (number_of - 1)
    while surplus > 0:
        movable = [i for i in range(1, number_of) if given[i] < largest] or [i for i in range(1, number_of) if given[i] < bound]
        pool, budget = sum([portions[i] for i in movable]), surplus
        for i in movable:
            more = min(bound - given[i], max(1, budget * portions[i] // pool), surplus)
            given[i] = given[i] + more
            surplus = surplus - more
    return np.array(given)


def centred(key, shape, scale, limit, shards=(), kind=jnp.bfloat16):
    loudness = shard_levels(key, shape, shards, -0.22, 0.18) if shards else 1.0
    drawn = jax.random.normal(key, shape, jnp.float32) * scale * loudness
    return jnp.minimum(jnp.maximum(drawn, -limit), limit).astype(kind)


def setup_inputs(seed: int = 0) -> dict:
    seeds = jax.random.split(jax.random.key(seed), 8)
    tokens = centred(seeds[0], (MICRO, TOKENS, D), 1.0, 6.0, ((1, 128),))
    routes_keys = jax.random.split(jax.random.fold_in(seeds[1], 1), MICRO * TOKENS // TOK_DEV)
    routes_turns = jax.random.permutation(jax.random.fold_in(seeds[1], 3), MICRO * TOKENS // TOK_DEV)
    routes = jax.vmap(lambda own, number: routed_block(jax.random.fold_in(seeds[1], 2), own, number, TOK_DEV, EXPERTS, TOP, CAP, 2))(routes_keys, routes_turns).reshape((MICRO, TOKENS, TOP))
    route_weights = jnp.clip(0.2 + 0.8 * jax.random.uniform(seeds[2], (MICRO, TOKENS, TOP), jnp.float32) ** shard_levels(seeds[2], (MICRO, TOKENS, TOP), ((1, 128),), -0.2, 0.2), 0.2, 1.0)
    slot_expert = draw_slot_expert(jax.random.fold_in(seeds[7], 71), 0)
    w_gate = draw_w_gate(jax.random.fold_in(seeds[7], 71), 0)
    w_up = draw_w_up(jax.random.fold_in(seeds[7], 71), 0)
    w_down = draw_w_down(jax.random.fold_in(seeds[7], 71), 0)
    return {"tokens": tokens, "routes": routes, "route_weights": route_weights, "slot_expert": slot_expert, "w_gate": w_gate, "w_up": w_up, "w_down": w_down}


def run_expert(row_block, gate_cols, up_cols, down_rows):
    gate_value = jnp.dot(row_block, gate_cols, preferred_element_type=jnp.float32)
    up_value = jnp.dot(row_block, up_cols, preferred_element_type=jnp.float32)
    hidden = (jax.nn.silu(gate_value) * up_value).astype(jnp.bfloat16)
    total = jnp.zeros((row_block.shape[0], D), jnp.float32)
    for group in range(HGROUPS):
        lower = group * QUART
        upper = lower + QUART
        partial_value = jnp.dot(hidden[:, lower:upper], down_rows[lower:upper], preferred_element_type=jnp.float32).astype(jnp.bfloat16)
        partial_value = lax.optimization_barrier(partial_value)
        total = total + partial_value.astype(jnp.float32)
    return total.astype(jnp.bfloat16)


def reference(tokens, routes, route_weights, slot_expert, w_gate, w_up, w_down):
    slot_ids = jnp.arange(SLOTS, dtype=jnp.int32)
    expert_ids = jnp.arange(EXPERTS, dtype=jnp.int32)
    primary = jnp.min(jnp.where(slot_expert[None, :] == expert_ids[:, None], slot_ids[None, :], SLOTS), axis=1).astype(jnp.int32)
    expert_rows = N_ATTN * N_EXPERT * CAP
    outputs = []
    for micro in range(MICRO):
        chosen = routes[micro].reshape(-1)
        token_rows = tokens[micro]

        def per_expert(carry, expert):
            ordering = jnp.argsort((chosen != expert).astype(jnp.int32), stable=True).astype(jnp.int32)[:expert_rows]
            valid = chosen[ordering] == expert
            row_block = jnp.where(valid[:, None], token_rows[ordering // TOP], jnp.zeros((), jnp.bfloat16))
            holder = primary[expert]
            result = run_expert(row_block, w_gate[holder], w_up[holder], w_down[holder])
            carry = carry.at[ordering].add(jnp.where(valid[:, None], result.astype(jnp.float32), jnp.zeros((), jnp.float32)))
            return carry, None

        start = jnp.zeros((TOKENS * TOP, D), jnp.float32)
        route_out, _ = lax.scan(per_expert, start, expert_ids)
        blended = jnp.sum(route_out.reshape(TOKENS, TOP, D) * route_weights[micro][:, :, None], axis=1)
        outputs.append(blended.astype(jnp.bfloat16))
    return jnp.stack(outputs)
```

```python
import jax
import jax.numpy as jnp
from jax import lax
from jax.experimental import pallas as pl
from jax.experimental.pallas import tpu as pltpu
from jax.sharding import Mesh, PartitionSpec as P


META = 128
TK = 1024
ORDERS = (("z", "y", "x"), ("y", "x", "z"), ("x", "z", "y"))


def gate_up_kernel(x_ref, wg_ref, wu_ref, pg_ref, pu_ref, coef_ref, h_ref, acc_ref):
    k = pl.program_id(0)
    rows = x_ref.shape[0]
    hid = wg_ref.shape[2]
    mats = (wg_ref, wu_ref, pg_ref, pu_ref)

    @pl.when(k == 0)
    def _():
        acc_ref[...] = jnp.zeros_like(acc_ref)

    @pl.loop(0, rows // 256)
    def _(r):
        here = pl.ds(pl.multiple_of(r * 256, 256), 256)
        x = x_ref[here, :]
        for m in range(4):
            for s in range(2):
                acc_ref[m * 2 + s, here, :] += jnp.dot(
                    x, mats[m][s], preferred_element_type=jnp.float32
                )

    @pl.when(k == pl.num_programs(0) - 1)
    def _():
        @pl.loop(0, rows // 256)
        def _(r):
            here = pl.ds(pl.multiple_of(r * 256, 256), 256)
            for side in range(2):
                for s in range(2):
                    g = acc_ref[side * 4 + s, here, :]
                    u = acc_ref[side * 4 + 2 + s, here, :]
                    j = side * 2 + s
                    c = coef_ref[here, j : j + 1]
                    v = jax.nn.silu(g) * u * c
                    h_ref[here, j * hid : (j + 1) * hid] = v.astype(jnp.bfloat16)


def gate_up(x, wg, wu, pg, pu, coef):
    rows = x.shape[0]
    depth, hid = wg.shape[1], wg.shape[2]
    wspec = pl.BlockSpec((2, TK, hid), lambda k: (0, k, 0))
    return pl.pallas_call(
        gate_up_kernel,
        grid=(depth // TK,),
        in_specs=[
            pl.BlockSpec((rows, TK), lambda k: (0, k)),
            wspec,
            wspec,
            wspec,
            wspec,
            pl.BlockSpec((rows, 4), lambda k: (0, 0)),
        ],
        out_specs=pl.BlockSpec((rows, 4 * hid), lambda k: (0, 0)),
        out_shape=jax.ShapeDtypeStruct((rows, 4 * hid), jnp.bfloat16),
        scratch_shapes=[pltpu.VMEM((8, rows, hid), jnp.float32)],
        compiler_params=pltpu.CompilerParams(
            dimension_semantics=("arbitrary",), vmem_limit_bytes=56 * 1024 * 1024
        ),
        cost_estimate=pl.CostEstimate(
            flops=2 * rows * depth * 8 * hid,
            bytes_accessed=2 * (rows * depth + 8 * depth * hid),
            transcendentals=rows * 4 * hid,
        ),
    )(x, wg, wu, pg, pu, coef)


def ring(axis):
    size = lax.axis_size(axis)
    return [
        (i * 2 + c, ((i + (1 if c == 0 else size - 1)) % size) * 2 + c)
        for i in range(size)
        for c in range(2)
    ]


def step(value, axis):
    return lax.ppermute(value, (axis, "c"), ring(axis))


def split_weights(w):
    hi = lax.reduce_precision(w, 8, 7)
    mid = lax.reduce_precision(w - hi, 8, 7)
    lo = lax.reduce_precision(w - hi - mid, 8, 7)
    return [v.astype(jnp.bfloat16) for v in (hi, mid, lo)]


def body(tokens, routes, route_weights, slot_expert, w_gate, w_up, w_down):
    micro, local_rows, width = tokens.shape
    top = routes.shape[2]
    slots = slot_expert.shape[0]
    per_device = w_gate.shape[0]
    core = lax.axis_index("c")
    sign = 1 - 2 * core
    sizes = {a: lax.axis_size(a) for a in "xyz"}

    swap = [(0, 1), (1, 0)]
    p_gate = lax.ppermute(w_gate, "c", swap)
    p_up = lax.ppermute(w_up, "c", swap)
    p_down = lax.ppermute(w_down, "c", swap)

    meta = [routes.astype(jnp.bfloat16)] + split_weights(route_weights)
    pad = jnp.zeros((micro, local_rows, META - 4 * top), jnp.bfloat16)
    sent = jnp.concatenate([tokens] + meta + [pad], axis=2)
    gathered = lax.all_gather(sent, ("x", "y", "z"), axis=1, tiled=True)
    rows = micro * gathered.shape[1]
    flat = gathered.reshape(rows, width + META)

    info = flat[:, width:].astype(jnp.float32)
    chosen = info[:, :top]
    weight = info[:, top : 2 * top] + info[:, 2 * top : 3 * top] + info[:, 3 * top : 4 * top]
    slot_ids = jnp.arange(slots, dtype=jnp.int32)
    same = slot_expert[:, None] == slot_expert[None, :]
    primary = ~jnp.any(same & (slot_ids[None, :] < slot_ids[:, None]), axis=1)
    held = jnp.where(primary, slot_expert, -1)
    chip = (lax.axis_index("y") * sizes["z"] + lax.axis_index("z")) * 2
    mine = lax.dynamic_slice(held, ((chip + core) * per_device,), (per_device,))
    theirs = lax.dynamic_slice(held, ((chip + 1 - core) * per_device,), (per_device,))
    local = jnp.concatenate([mine, theirs]).astype(jnp.float32)
    hit = chosen[:, None, :] == local[None, :, None]
    coef = jnp.sum(jnp.where(hit, weight[:, None, :], 0.0), axis=2)

    hidden = gate_up(flat, w_gate, w_up, p_gate, p_up, coef)
    depth = hidden.shape[1] // 2
    grid = hidden.reshape(micro, sizes["x"], sizes["y"], sizes["z"], local_rows, 2 * depth)
    down_own = w_down.reshape(depth, width)
    down_other = p_down.reshape(depth, width)

    lanes = width // 128
    cuts = [0, (lanes + 2) // 3 * 128, 2 * ((lanes + 2) // 3) * 128, width]
    finals = []
    for color, order in enumerate(ORDERS):
        lower, upper = cuts[color], cuts[color + 1]
        own_cols, other_cols = down_own[:, lower:upper], down_other[:, lower:upper]
        names = ["x", "y", "z"]
        held_sum = None
        for stage, axis in enumerate(order):
            dim = 1 + names.index(axis)
            here = lax.axis_index(axis)
            size = sizes[axis]

            def take(offset):
                at = lax.rem(here - sign * offset + 2 * size, size)
                if stage == 0:
                    part = lax.dynamic_index_in_dim(grid, at, dim, keepdims=False)
                    shape = part.shape[:-1]
                    part = part.reshape(-1, 2 * depth)
                    value = jnp.dot(
                        part[:, :depth], own_cols, preferred_element_type=jnp.float32
                    ) + jnp.dot(
                        part[:, depth:], other_cols, preferred_element_type=jnp.float32
                    )
                    return value.reshape(shape + (upper - lower,))
                return lax.dynamic_index_in_dim(held_sum, at, dim, keepdims=False).astype(
                    jnp.float32
                )

            moving = take(1).astype(jnp.bfloat16)
            for hop in range(2, size + 1):
                moving = step(moving, axis)
                moving = (moving.astype(jnp.float32) + take(hop)).astype(jnp.bfloat16)
            held_sum = moving
            names.remove(axis)
        finals.append(held_sum)
    return jnp.concatenate(finals, axis=2)


def solution(mesh):
    fine = Mesh(mesh.devices.reshape(4, 4, 4, 2), ("x", "y", "z", "c"))
    row = P(None, ("x", "y", "z", "c"), None)
    column = P(("y", "z", "c"), None, "x")
    in_specs = (row, row, row, P(), column, column, P(("y", "z", "c"), "x", None))
    return jax.shard_map(body, mesh=fine, in_specs=in_specs, out_specs=row, check_vma=False)
```

```python
import jax
import jax.numpy as jnp
from jax import lax
from jax.experimental import pallas as pl
from jax.experimental.pallas import tpu as pltpu
from jax.sharding import Mesh, PartitionSpec as P


META = 128
TK = 1024
TOP = 8
GROUP = 8
CAP = 2
BLOCK = 256
SEATS = BLOCK // GROUP * CAP
ORDERS = (("z", "y", "x"), ("y", "x", "z"), ("x", "z", "y"))


def gate_up_kernel(
    local_ref, x_ref, meta_ref, wg_ref, wu_ref, pg_ref, pu_ref, h_ref, acc, packed, select, scale
):
    k = pl.program_id(0)
    rows, _ = x_ref.shape
    hid = wg_ref.shape[2]
    blocks = rows // BLOCK
    top = TOP

    @pl.when(k == 0)
    def _():
        acc[...] = jnp.zeros_like(acc)
        early = lax.broadcasted_iota(jnp.int32, (BLOCK, BLOCK), 0)
        late = lax.broadcasted_iota(jnp.int32, (BLOCK, BLOCK), 1)
        before = ((early < late) & (early // GROUP == late // GROUP)).astype(jnp.bfloat16)
        place = lax.broadcasted_iota(jnp.int32, (SEATS, BLOCK), 0).astype(jnp.float32)
        group = lax.broadcasted_iota(jnp.int32, (1, BLOCK), 1) // GROUP
        seat0 = (group * CAP).astype(jnp.float32)
        for b in range(blocks):
            info = meta_ref[b * BLOCK : (b + 1) * BLOCK, :].astype(jnp.float32).T
            chosen = info[:top]
            weight = info[top : 2 * top] + info[2 * top : 3 * top] + info[3 * top : 4 * top]
            for j in range(4):
                hit = chosen == local_ref[j]
                coef = jnp.sum(jnp.where(hit, weight, 0.0), axis=0, keepdims=True)
                active = jnp.sum(jnp.where(hit, 1.0, 0.0), axis=0, keepdims=True)
                earlier = jnp.dot(
                    jnp.broadcast_to(active, (8, BLOCK)).astype(jnp.bfloat16),
                    before,
                    preferred_element_type=jnp.float32,
                )[:1]
                seat = jnp.where(active > 0.5, seat0 + earlier, -1.0)
                taken = place == seat
                select[b, j * SEATS : (j + 1) * SEATS, :] = jnp.where(taken, 1.0, 0.0).astype(
                    jnp.bfloat16
                )
                picked = jnp.sum(jnp.where(taken, coef, 0.0), axis=1, keepdims=True)
                scale[j, b * SEATS : (b + 1) * SEATS, :] = jnp.broadcast_to(picked, (SEATS, 128))

    for b in range(blocks):
        got = jnp.dot(
            select[b], x_ref[b * BLOCK : (b + 1) * BLOCK, :], preferred_element_type=jnp.float32
        ).astype(jnp.bfloat16)
        for j in range(4):
            packed[j, b * SEATS : (b + 1) * SEATS, :] = got[j * SEATS : (j + 1) * SEATS]
    for j in range(4):
        gate_w, up_w = ((wg_ref, wu_ref), (pg_ref, pu_ref))[j // 2]
        x = packed[j]
        acc[j, 0] += jnp.dot(x, gate_w[j % 2], preferred_element_type=jnp.float32)
        acc[j, 1] += jnp.dot(x, up_w[j % 2], preferred_element_type=jnp.float32)

    @pl.when(k == pl.num_programs(0) - 1)
    def _():
        for j in range(4):
            value = jax.nn.silu(acc[j, 0]) * acc[j, 1] * scale[j, :, :1]
            value = value.astype(jnp.bfloat16)
            for b in range(blocks):
                spread = select[b, j * SEATS : (j + 1) * SEATS, :].astype(jnp.float32).T
                h_ref[b * BLOCK : (b + 1) * BLOCK, j * hid : (j + 1) * hid] = jnp.dot(
                    spread.astype(jnp.bfloat16),
                    value[b * SEATS : (b + 1) * SEATS],
                    preferred_element_type=jnp.float32,
                ).astype(jnp.bfloat16)


def gate_up(local, x, wg, wu, pg, pu):
    rows = x.shape[0]
    depth, hid = wg.shape[1], wg.shape[2]
    packed_rows = rows // BLOCK * SEATS
    wspec = pl.BlockSpec((2, TK, hid), lambda k: (0, k, 0))
    return pl.pallas_call(
        gate_up_kernel,
        grid=(depth // TK,),
        in_specs=[
            pl.BlockSpec(memory_space=pltpu.SMEM),
            pl.BlockSpec((rows, TK), lambda k: (0, k)),
            pl.BlockSpec((rows, META), lambda k: (0, depth // META)),
            wspec,
            wspec,
            wspec,
            wspec,
        ],
        out_specs=pl.BlockSpec((rows, 4 * hid), lambda k: (0, 0)),
        out_shape=jax.ShapeDtypeStruct((rows, 4 * hid), jnp.bfloat16),
        scratch_shapes=[
            pltpu.VMEM((4, 2, packed_rows, hid), jnp.float32),
            pltpu.VMEM((4, packed_rows, TK), jnp.bfloat16),
            pltpu.VMEM((rows // BLOCK, 4 * SEATS, BLOCK), jnp.bfloat16),
            pltpu.VMEM((4, packed_rows, 128), jnp.float32),
        ],
        compiler_params=pltpu.CompilerParams(
            dimension_semantics=("arbitrary",), vmem_limit_bytes=40 * 1024 * 1024
        ),
        cost_estimate=pl.CostEstimate(
            flops=2 * packed_rows * depth * 8 * hid,
            bytes_accessed=2 * (rows * depth + 8 * depth * hid),
            transcendentals=packed_rows * 4 * hid,
        ),
    )(local, x, x, wg, wu, pg, pu)


def shift(value, axis, by):
    size = lax.axis_size(axis)
    return lax.ppermute(value, axis, [(i, (i + by) % size) for i in range(size)])


def split_weights(w):
    hi = lax.reduce_precision(w, 8, 7)
    mid = lax.reduce_precision(w - hi, 8, 7)
    lo = lax.reduce_precision(w - hi - mid, 8, 7)
    return [v.astype(jnp.bfloat16) for v in (hi, mid, lo)]


def body(tokens, routes, route_weights, slot_expert, w_gate, w_up, w_down):
    micro, local_rows, width = tokens.shape
    slots = slot_expert.shape[0]
    per_device = w_gate.shape[0]
    core = lax.axis_index("c")
    sizes = {a: lax.axis_size(a) for a in "xyz"}
    half = jnp.bfloat16

    swap = [(0, 1), (1, 0)]
    p_gate = lax.ppermute(w_gate, "c", swap)
    p_up = lax.ppermute(w_up, "c", swap)
    p_down = lax.ppermute(w_down, "c", swap)

    meta = [routes.astype(half)] + split_weights(route_weights)
    pad = jnp.zeros((micro, local_rows, META - 4 * TOP), half)
    sent = jnp.concatenate([tokens] + meta + [pad], axis=2)
    sent = sent.reshape(micro * local_rows, width + META)
    gathered = lax.all_gather(sent, ("x", "y", "z"), axis=0, tiled=True)

    slot_ids = jnp.arange(slots, dtype=jnp.int32)
    same = slot_expert[:, None] == slot_expert[None, :]
    primary = ~jnp.any(same & (slot_ids[None, :] < slot_ids[:, None]), axis=1)
    held = jnp.where(primary, slot_expert, -1)
    chip = (lax.axis_index("y") * sizes["z"] + lax.axis_index("z")) * 2
    mine = lax.dynamic_slice(held, ((chip + core) * per_device,), (per_device,))
    theirs = lax.dynamic_slice(held, ((chip + 1 - core) * per_device,), (per_device,))
    local = jnp.concatenate([mine, theirs]).astype(jnp.float32)

    down_rows = per_device * w_down.shape[1]
    lanes = width // 128
    cuts = [0, (lanes + 2) // 3 * 128, 2 * ((lanes + 2) // 3) * 128, width]
    downs = [
        jnp.concatenate(
            [v.reshape(down_rows, width)[:, cuts[c] : cuts[c + 1]] for v in (w_down, p_down)]
        )
        for c in range(3)
    ]
    gathered, downs, local = lax.optimization_barrier((gathered, downs, local))

    hidden = gate_up(local, gathered, w_gate, w_up, p_gate, p_up)
    grid = hidden.reshape(
        sizes["x"], sizes["y"], sizes["z"], micro * local_rows, hidden.shape[1]
    )

    def chunk(array, axis, offset, names):
        at = lax.rem(lax.axis_index(axis) + offset + sizes[axis], sizes[axis])
        return lax.dynamic_index_in_dim(array, at, names.index(axis), keepdims=False)

    def project(color, upper, lower):
        mid = upper.shape[0] // 2
        part = jnp.concatenate([upper[:mid], lower[mid:]]) if upper is not lower else upper
        value = jnp.dot(
            part.reshape(-1, part.shape[-1]), downs[color], preferred_element_type=jnp.float32
        )
        return value.reshape(part.shape[:-1] + (value.shape[-1],))

    first = [order[0] for order in ORDERS]
    outs = []
    for color, axis in enumerate(first):
        far = chunk(grid, axis, 2, "xyz")
        up = project(color, far, chunk(grid, axis, 1, "xyz")).astype(half)
        down = project(color, chunk(grid, axis, -1, "xyz"), far).astype(half)
        outs.append((up, down))
    grid, outs = lax.optimization_barrier((grid, outs))
    got = [(shift(up, axis, 1), shift(down, axis, -1)) for (up, down), axis in zip(outs, first)]
    last = []
    for color, axis in enumerate(first):
        mine_mid = project(color, chunk(grid, axis, 1, "xyz"), chunk(grid, axis, -1, "xyz"))
        mid = mine_mid.shape[0] // 2
        up, down = got[color]
        near_up = (mine_mid[:mid] + up[:mid].astype(jnp.float32)).astype(half)
        near_down = (mine_mid[mid:] + down[mid:].astype(jnp.float32)).astype(half)
        last.append((shift(near_up, axis, 1), shift(near_down, axis, -1)))
    sums = []
    for color, axis in enumerate(first):
        here = chunk(grid, axis, 0, "xyz")
        own = project(color, here, here)
        mid = own.shape[0] // 2
        up, down = [v.astype(jnp.float32) for v in got[color]]
        up2, down2 = [v.astype(jnp.float32) for v in last[color]]
        sums.append(
            jnp.concatenate([own[:mid] + up2 + down[:mid], own[mid:] + up[mid:] + down2])
        )
    names = ["xyz".replace(axis, "") for axis in first]
    for stage in (1, 2):
        arrived = []
        for color in range(3):
            axis = ORDERS[color][stage]
            arrived.append(
                [
                    shift(chunk(sums[color], axis, offset, names[color]).astype(half), axis, offset)
                    for offset in (1, -1, 2)
                ]
            )
        for color in range(3):
            axis = ORDERS[color][stage]
            total = chunk(sums[color], axis, 0, names[color])
            for piece in arrived[color]:
                total = total + piece.astype(jnp.float32)
            sums[color] = total
            names[color] = names[color].replace(axis, "")
    result = jnp.concatenate([v.astype(half) for v in sums], axis=1)
    return result.reshape(micro, local_rows, width)


def solution(mesh):
    fine = Mesh(mesh.devices.reshape(4, 4, 4, 2), ("x", "y", "z", "c"))
    row = P(None, ("x", "y", "z", "c"), None)
    column = P(("y", "z", "c"), None, "x")
    in_specs = (row, row, row, P(), column, column, P(("y", "z", "c"), "x", None))
    return jax.shard_map(body, mesh=fine, in_specs=in_specs, out_specs=row, check_vma=False)
```

```python
import jax
import jax.numpy as jnp
from jax import lax
from jax.experimental import pallas as pl
from jax.experimental.pallas import tpu as pltpu
from jax.sharding import Mesh, PartitionSpec as P


META = 128
TK = 512
TOP = 8
GROUP = 8
CAP = 2
BLOCK = 256
SEATS = BLOCK // GROUP * CAP
ORDERS = (("z", "y", "x"), ("y", "x", "z"), ("x", "z", "y"))


def gate_up_kernel(
    local_ref, x_ref, meta_ref, wg_ref, wu_ref, pg_ref, pu_ref, h_ref, acc, packed, select, scale
):
    k = pl.program_id(0)
    rows, _ = x_ref.shape
    hid = wg_ref.shape[2]
    blocks = rows // BLOCK
    top = TOP

    @pl.when(k == 0)
    def _():
        acc[...] = jnp.zeros_like(acc)
        early = lax.broadcasted_iota(jnp.int32, (BLOCK, BLOCK), 0)
        late = lax.broadcasted_iota(jnp.int32, (BLOCK, BLOCK), 1)
        before = ((early < late) & (early // GROUP == late // GROUP)).astype(jnp.bfloat16)
        place = lax.broadcasted_iota(jnp.int32, (SEATS, BLOCK), 0).astype(jnp.float32)
        group = lax.broadcasted_iota(jnp.int32, (1, BLOCK), 1) // GROUP
        seat0 = (group * CAP).astype(jnp.float32)

        @pl.loop(0, blocks)
        def _(b):
            here = pl.ds(pl.multiple_of(b * BLOCK, BLOCK), BLOCK)
            seats = pl.ds(pl.multiple_of(b * SEATS, SEATS), SEATS)
            info = meta_ref[here, :].astype(jnp.float32).T
            chosen = info[:top]
            weight = info[top : 2 * top] + info[2 * top : 3 * top] + info[3 * top : 4 * top]
            for j in range(4):
                hit = chosen == local_ref[j]
                coef = jnp.sum(jnp.where(hit, weight, 0.0), axis=0, keepdims=True)
                active = jnp.sum(jnp.where(hit, 1.0, 0.0), axis=0, keepdims=True)
                earlier = jnp.dot(
                    jnp.broadcast_to(active, (8, BLOCK)).astype(jnp.bfloat16),
                    before,
                    preferred_element_type=jnp.float32,
                )[:1]
                seat = jnp.where(active > 0.5, seat0 + earlier, -1.0)
                taken = place == seat
                select[b, j * SEATS : (j + 1) * SEATS, :] = jnp.where(taken, 1.0, 0.0).astype(
                    jnp.bfloat16
                )
                picked = jnp.sum(jnp.where(taken, coef, 0.0), axis=1, keepdims=True)
                scale[j, seats, :] = jnp.broadcast_to(picked, (SEATS, 128))

    @pl.loop(0, blocks)
    def _(b):
        here = pl.ds(pl.multiple_of(b * BLOCK, BLOCK), BLOCK)
        got = jnp.dot(select[b], x_ref[here, :], preferred_element_type=jnp.float32)
        got = got.astype(jnp.bfloat16)
        seats = pl.ds(pl.multiple_of(b * SEATS, SEATS), SEATS)
        for j in range(4):
            packed[j, seats, :] = got[j * SEATS : (j + 1) * SEATS]

    for side, (gate_w, up_w) in enumerate(((wg_ref, wu_ref), (pg_ref, pu_ref))):

        @pl.loop(0, 2)
        def _(i):
            j = side * 2 + i
            x = packed[j]
            acc[j, 0] += jnp.dot(x, gate_w[i], preferred_element_type=jnp.float32)
            acc[j, 1] += jnp.dot(x, up_w[i], preferred_element_type=jnp.float32)

    @pl.when(k == pl.num_programs(0) - 1)
    def _():

        @pl.loop(0, 4)
        def _(j):
            value = jax.nn.silu(acc[j, 0]) * acc[j, 1] * scale[j, :, :1]
            value = value.astype(jnp.bfloat16)
            columns = pl.ds(pl.multiple_of(j * hid, hid), hid)
            seats = pl.ds(pl.multiple_of(j * SEATS, SEATS), SEATS)
            for b in range(blocks):
                spread = select[b, seats, :].astype(jnp.float32).T
                h_ref[b * BLOCK : (b + 1) * BLOCK, columns] = jnp.dot(
                    spread.astype(jnp.bfloat16),
                    value[b * SEATS : (b + 1) * SEATS],
                    preferred_element_type=jnp.float32,
                ).astype(jnp.bfloat16)


def gate_up(local, x, wg, wu, pg, pu):
    rows = x.shape[0]
    depth, hid = wg.shape[1], wg.shape[2]
    packed_rows = rows // BLOCK * SEATS
    wspec = pl.BlockSpec((2, TK, hid), lambda k: (0, k, 0))
    return pl.pallas_call(
        gate_up_kernel,
        grid=(depth // TK,),
        in_specs=[
            pl.BlockSpec(memory_space=pltpu.SMEM),
            pl.BlockSpec((rows, TK), lambda k: (0, k)),
            pl.BlockSpec((rows, META), lambda k: (0, depth // META)),
            wspec,
            wspec,
            wspec,
            wspec,
        ],
        out_specs=pl.BlockSpec((rows, 4 * hid), lambda k: (0, 0)),
        out_shape=jax.ShapeDtypeStruct((rows, 4 * hid), jnp.bfloat16),
        scratch_shapes=[
            pltpu.VMEM((4, 2, packed_rows, hid), jnp.float32),
            pltpu.VMEM((4, packed_rows, TK), jnp.bfloat16),
            pltpu.VMEM((rows // BLOCK, 4 * SEATS, BLOCK), jnp.bfloat16),
            pltpu.VMEM((4, packed_rows, 128), jnp.float32),
        ],
        compiler_params=pltpu.CompilerParams(
            dimension_semantics=("arbitrary",), vmem_limit_bytes=40 * 1024 * 1024
        ),
        cost_estimate=pl.CostEstimate(
            flops=2 * packed_rows * depth * 8 * hid,
            bytes_accessed=2 * (rows * depth + 8 * depth * hid),
            transcendentals=packed_rows * 4 * hid,
        ),
    )(local, x, x, wg, wu, pg, pu)


def join_kernel(own_ref, other_ref, out_ref):
    rows = own_ref.shape[0]
    out_ref[:rows] = own_ref[...]
    out_ref[rows:] = other_ref[...]


def join(own, other, lower, upper):
    rows = own.shape[0]
    first = lower // 128
    source = pl.BlockSpec((rows, 128), lambda n: (0, first + n))
    return pl.pallas_call(
        join_kernel,
        grid=((upper - lower) // 128,),
        in_specs=[source, source],
        out_specs=pl.BlockSpec((2 * rows, 128), lambda n: (0, n)),
        out_shape=jax.ShapeDtypeStruct((2 * rows, upper - lower), own.dtype),
        cost_estimate=pl.CostEstimate(
            flops=0, bytes_accessed=8 * rows * (upper - lower), transcendentals=0
        ),
    )(own, other)


def shift(value, axis, by):
    size = lax.axis_size(axis)
    return lax.ppermute(value, axis, [(i, (i + by) % size) for i in range(size)])


def split_weights(w):
    hi = lax.reduce_precision(w, 8, 7)
    mid = lax.reduce_precision(w - hi, 8, 7)
    lo = lax.reduce_precision(w - hi - mid, 8, 7)
    return [v.astype(jnp.bfloat16) for v in (hi, mid, lo)]


def body(tokens, routes, route_weights, slot_expert, w_gate, w_up, w_down):
    micro, local_rows, width = tokens.shape
    slots = slot_expert.shape[0]
    per_device = w_gate.shape[0]
    core = lax.axis_index("c")
    sizes = {a: lax.axis_size(a) for a in "xyz"}
    half = jnp.bfloat16

    swap = [(0, 1), (1, 0)]
    p_gate = lax.ppermute(w_gate, "c", swap)
    p_up = lax.ppermute(w_up, "c", swap)
    p_down = lax.ppermute(w_down, "c", swap)

    meta = [routes.astype(half)] + split_weights(route_weights)
    pad = jnp.zeros((micro, local_rows, META - 4 * TOP), half)
    sent = jnp.concatenate([tokens] + meta + [pad], axis=2)
    sent = sent.reshape(micro * local_rows, width + META)
    gathered = lax.all_gather(sent, ("x", "y", "z"), axis=0, tiled=True)

    slot_ids = jnp.arange(slots, dtype=jnp.int32)
    same = slot_expert[:, None] == slot_expert[None, :]
    primary = ~jnp.any(same & (slot_ids[None, :] < slot_ids[:, None]), axis=1)
    held = jnp.where(primary, slot_expert, -1)
    chip = (lax.axis_index("y") * sizes["z"] + lax.axis_index("z")) * 2
    mine = lax.dynamic_slice(held, ((chip + core) * per_device,), (per_device,))
    theirs = lax.dynamic_slice(held, ((chip + 1 - core) * per_device,), (per_device,))
    local = jnp.concatenate([mine, theirs]).astype(jnp.float32)

    down_rows = per_device * w_down.shape[1]
    lanes = width // 128
    wide = (lanes + 2) // 3 * 128
    cuts = [0, width - 2 * wide, width - wide, width]
    flat_own, flat_other = w_down.reshape(down_rows, width), p_down.reshape(down_rows, width)
    downs = [join(flat_own, flat_other, cuts[c], cuts[c + 1]) for c in range(3)]
    gathered, downs, local = lax.optimization_barrier((gathered, downs, local))

    hidden = gate_up(local, gathered, w_gate, w_up, p_gate, p_up)
    grid = hidden.reshape(
        sizes["x"], sizes["y"], sizes["z"], micro * local_rows, hidden.shape[1]
    )

    def chunk(array, axis, offset, names):
        at = lax.rem(lax.axis_index(axis) + offset + sizes[axis], sizes[axis])
        return lax.dynamic_index_in_dim(array, at, names.index(axis), keepdims=False)

    def project(color, upper, lower):
        mid = upper.shape[0] // 2
        part = jnp.concatenate([upper[:mid], lower[mid:]]) if upper is not lower else upper
        value = jnp.dot(
            part.reshape(-1, part.shape[-1]), downs[color], preferred_element_type=jnp.float32
        )
        return value.reshape(part.shape[:-1] + (value.shape[-1],))

    first = [order[0] for order in ORDERS]
    got = []
    for color, axis in enumerate(first):
        far = chunk(grid, axis, 2, "xyz")
        up = project(color, far, chunk(grid, axis, 1, "xyz")).astype(half)
        down = project(color, chunk(grid, axis, -1, "xyz"), far).astype(half)
        got.append((shift(up, axis, 1), shift(down, axis, -1)))
        grid, _, _ = lax.optimization_barrier((grid, up, down))
    last = []
    for color, axis in enumerate(first):
        mine_mid = project(color, chunk(grid, axis, 1, "xyz"), chunk(grid, axis, -1, "xyz"))
        mid = mine_mid.shape[0] // 2
        up, down = got[color]
        near_up = (mine_mid[:mid] + up[:mid].astype(jnp.float32)).astype(half)
        near_down = (mine_mid[mid:] + down[mid:].astype(jnp.float32)).astype(half)
        last.append((shift(near_up, axis, 1), shift(near_down, axis, -1)))
    sums = []
    for color, axis in enumerate(first):
        here = chunk(grid, axis, 0, "xyz")
        own = project(color, here, here)
        mid = own.shape[0] // 2
        up, down = [v.astype(jnp.float32) for v in got[color]]
        up2, down2 = [v.astype(jnp.float32) for v in last[color]]
        sums.append(
            jnp.concatenate([own[:mid] + up2 + down[:mid], own[mid:] + up[mid:] + down2])
        )
    names = ["xyz".replace(axis, "") for axis in first]
    for stage in (1, 2):
        arrived = []
        for color in range(3):
            axis = ORDERS[color][stage]
            arrived.append(
                [
                    shift(chunk(sums[color], axis, offset, names[color]).astype(half), axis, offset)
                    for offset in (1, -1, 2)
                ]
            )
        for color in range(3):
            axis = ORDERS[color][stage]
            total = chunk(sums[color], axis, 0, names[color])
            for piece in arrived[color]:
                total = total + piece.astype(jnp.float32)
            sums[color] = total
            names[color] = names[color].replace(axis, "")
    result = jnp.concatenate([v.astype(half) for v in sums], axis=1)
    return result.reshape(micro, local_rows, width)


def solution(mesh):
    fine = Mesh(mesh.devices.reshape(4, 4, 4, 2), ("x", "y", "z", "c"))
    row = P(None, ("x", "y", "z", "c"), None)
    column = P(("y", "z", "c"), None, "x")
    in_specs = (row, row, row, P(), column, column, P(("y", "z", "c"), "x", None))
    return jax.shard_map(body, mesh=fine, in_specs=in_specs, out_specs=row, check_vma=False)
```

```python
import functools

import jax
import jax.numpy as jnp
from jax import lax
from jax.experimental import pallas as pl
from jax.experimental.pallas import tpu as pltpu
from jax.sharding import Mesh, PartitionSpec as P


META = 128
TK = 1024
TOP = 8
GROUP = 8
CAP = 2
BLOCK = 256
SEATS = BLOCK // GROUP * CAP
ORDERS = (("z", "y", "x"), ("y", "x", "z"), ("x", "z", "y"))


def gate_up_kernel(
    local_ref, x_ref, meta_ref, wg_ref, wu_ref, pg_ref, pu_ref, h_ref, acc, packed, select, scale
):
    k = pl.program_id(0)
    rows, _ = x_ref.shape
    hid = wg_ref.shape[2]
    blocks = rows // BLOCK
    top = TOP

    @pl.when(k == 0)
    def _():
        acc[...] = jnp.zeros_like(acc)
        early = lax.broadcasted_iota(jnp.int32, (BLOCK, BLOCK), 0)
        late = lax.broadcasted_iota(jnp.int32, (BLOCK, BLOCK), 1)
        before = ((early < late) & (early // GROUP == late // GROUP)).astype(jnp.bfloat16)
        place = lax.broadcasted_iota(jnp.int32, (SEATS, BLOCK), 0).astype(jnp.float32)
        group = lax.broadcasted_iota(jnp.int32, (1, BLOCK), 1) // GROUP
        seat0 = (group * CAP).astype(jnp.float32)

        @pl.loop(0, blocks)
        def _(b):
            here = pl.ds(pl.multiple_of(b * BLOCK, BLOCK), BLOCK)
            seats = pl.ds(pl.multiple_of(b * SEATS, SEATS), SEATS)
            info = meta_ref[here, :].astype(jnp.float32).T
            chosen = info[:top]
            weight = info[top : 2 * top] + info[2 * top : 3 * top] + info[3 * top : 4 * top]
            for j in range(4):
                hit = chosen == local_ref[j]
                coef = jnp.sum(jnp.where(hit, weight, 0.0), axis=0, keepdims=True)
                active = jnp.sum(jnp.where(hit, 1.0, 0.0), axis=0, keepdims=True)
                earlier = jnp.dot(
                    jnp.broadcast_to(active, (8, BLOCK)).astype(jnp.bfloat16),
                    before,
                    preferred_element_type=jnp.float32,
                )[:1]
                seat = jnp.where(active > 0.5, seat0 + earlier, -1.0)
                taken = place == seat
                select[b, j * SEATS : (j + 1) * SEATS, :] = jnp.where(taken, 1.0, 0.0).astype(
                    jnp.bfloat16
                )
                picked = jnp.sum(jnp.where(taken, coef, 0.0), axis=1, keepdims=True)
                scale[j, seats, :] = jnp.broadcast_to(picked, (SEATS, 128))

    for b in range(blocks):
        got = jnp.dot(
            select[b], x_ref[b * BLOCK : (b + 1) * BLOCK, :], preferred_element_type=jnp.float32
        ).astype(jnp.bfloat16)
        for j in range(4):
            packed[j, b * SEATS : (b + 1) * SEATS, :] = got[j * SEATS : (j + 1) * SEATS]
    for j in range(4):
        gate_w, up_w = ((wg_ref, wu_ref), (pg_ref, pu_ref))[j // 2]
        x = packed[j]
        acc[j, 0] += jnp.dot(x, gate_w[j % 2], preferred_element_type=jnp.float32)
        acc[j, 1] += jnp.dot(x, up_w[j % 2], preferred_element_type=jnp.float32)

    @pl.when(k == pl.num_programs(0) - 1)
    def _():

        @pl.loop(0, 4)
        def _(j):
            value = jax.nn.silu(acc[j, 0]) * acc[j, 1] * scale[j, :, :1]
            value = value.astype(jnp.bfloat16)
            columns = pl.ds(pl.multiple_of(j * hid, hid), hid)
            seats = pl.ds(pl.multiple_of(j * SEATS, SEATS), SEATS)
            for b in range(blocks):
                spread = select[b, seats, :].astype(jnp.float32).T
                h_ref[b * BLOCK : (b + 1) * BLOCK, columns] = jnp.dot(
                    spread.astype(jnp.bfloat16),
                    value[b * SEATS : (b + 1) * SEATS],
                    preferred_element_type=jnp.float32,
                ).astype(jnp.bfloat16)


def gate_up(local, x, wg, wu, pg, pu):
    rows = x.shape[0]
    depth, hid = wg.shape[1], wg.shape[2]
    packed_rows = rows // BLOCK * SEATS
    wspec = pl.BlockSpec((2, TK, hid), lambda k: (0, k, 0))
    return pl.pallas_call(
        gate_up_kernel,
        grid=(depth // TK,),
        in_specs=[
            pl.BlockSpec(memory_space=pltpu.SMEM),
            pl.BlockSpec((rows, TK), lambda k: (0, k)),
            pl.BlockSpec((rows, META), lambda k: (0, depth // META)),
            wspec,
            wspec,
            wspec,
            wspec,
        ],
        out_specs=pl.BlockSpec((rows, 4 * hid), lambda k: (0, 0)),
        out_shape=jax.ShapeDtypeStruct((rows, 4 * hid), jnp.bfloat16),
        scratch_shapes=[
            pltpu.VMEM((4, 2, packed_rows, hid), jnp.float32),
            pltpu.VMEM((4, packed_rows, TK), jnp.bfloat16),
            pltpu.VMEM((rows // BLOCK, 4 * SEATS, BLOCK), jnp.bfloat16),
            pltpu.VMEM((4, packed_rows, 128), jnp.float32),
        ],
        compiler_params=pltpu.CompilerParams(
            dimension_semantics=("arbitrary",), vmem_limit_bytes=60 * 1024 * 1024
        ),
        cost_estimate=pl.CostEstimate(
            flops=2 * packed_rows * depth * 8 * hid,
            bytes_accessed=2 * (rows * depth + 8 * depth * hid),
            transcendentals=packed_rows * 4 * hid,
        ),
    )(local, x, x, wg, wu, pg, pu)


def join_kernel(own_ref, other_ref, out_ref):
    rows = own_ref.shape[0]
    out_ref[:rows] = own_ref[...]
    out_ref[rows:] = other_ref[...]


def join(own, other, lower, upper):
    rows = own.shape[0]
    first = lower // 128
    source = pl.BlockSpec((rows, 128), lambda n: (0, first + n))
    return pl.pallas_call(
        join_kernel,
        grid=((upper - lower) // 128,),
        in_specs=[source, source],
        out_specs=pl.BlockSpec((2 * rows, 128), lambda n: (0, n)),
        out_shape=jax.ShapeDtypeStruct((2 * rows, upper - lower), own.dtype),
        cost_estimate=pl.CostEstimate(
            flops=0, bytes_accessed=8 * rows * (upper - lower), transcendentals=0
        ),
    )(own, other)


def project_kernel(dim, picks, at_ref, h_ref, w_ref, *refs):
    outs, rows_ref = refs[:-1], refs[-1]
    lead = h_ref.shape[0] // 2

    @pl.when(pl.program_id(0) == 0)
    def _():
        start = 0
        for pair in picks:
            for side, pick in enumerate(pair):
                at = at_ref[pick]
                lo = side * lead
                if dim == 0:
                    part = h_ref[at, lo : lo + lead]
                elif dim == 1:
                    part = h_ref[lo : lo + lead, at]
                else:
                    part = h_ref[lo : lo + lead, :, at]
                part = part.reshape(-1, h_ref.shape[-1])
                rows_ref[start : start + part.shape[0]] = part
                start += part.shape[0]

    count = rows_ref.shape[0] // len(outs)
    for n, out in enumerate(outs):
        value = jnp.dot(
            rows_ref[n * count : (n + 1) * count], w_ref[...], preferred_element_type=jnp.float32
        )
        out[...] = value.astype(out.dtype).reshape(out.shape)


def project(grid, weights, at, dim, picks, dtype):
    size, depth = grid.shape[0], grid.shape[-1]
    rest = [n for i, n in enumerate(grid.shape[:3]) if i != dim] + [grid.shape[3]]
    columns = weights.shape[1]
    rows = rest[0] * rest[1] * rest[2]
    return pl.pallas_call(
        functools.partial(project_kernel, dim, picks),
        grid=(columns // BLOCK,),
        in_specs=[
            pl.BlockSpec(memory_space=pltpu.SMEM),
            pl.BlockSpec(grid.shape, lambda n: (0, 0, 0, 0, 0)),
            pl.BlockSpec((depth, BLOCK), lambda n: (0, n)),
        ],
        out_specs=[pl.BlockSpec((*rest, BLOCK), lambda n: (0, 0, 0, n))] * len(picks),
        out_shape=[jax.ShapeDtypeStruct((*rest, columns), dtype)] * len(picks),
        scratch_shapes=[pltpu.VMEM((rows * len(picks), depth), jnp.bfloat16)],
        compiler_params=pltpu.CompilerParams(
            dimension_semantics=("arbitrary",), vmem_limit_bytes=24 * 1024 * 1024
        ),
        cost_estimate=pl.CostEstimate(
            flops=2 * rows * len(picks) * depth * columns,
            bytes_accessed=2 * depth * columns,
            transcendentals=0,
        ),
    )(at, grid, weights)


def shift(value, axis, by):
    size = lax.axis_size(axis)
    return lax.ppermute(value, axis, [(i, (i + by) % size) for i in range(size)])


def split_weights(w):
    hi = lax.reduce_precision(w, 8, 7)
    mid = lax.reduce_precision(w - hi, 8, 7)
    lo = lax.reduce_precision(w - hi - mid, 8, 7)
    return [v.astype(jnp.bfloat16) for v in (hi, mid, lo)]


def body(tokens, routes, route_weights, slot_expert, w_gate, w_up, w_down):
    micro, local_rows, width = tokens.shape
    slots = slot_expert.shape[0]
    per_device = w_gate.shape[0]
    core = lax.axis_index("c")
    sizes = {a: lax.axis_size(a) for a in "xyz"}
    half = jnp.bfloat16

    swap = [(0, 1), (1, 0)]
    p_gate = lax.ppermute(w_gate, "c", swap)
    p_up = lax.ppermute(w_up, "c", swap)
    p_down = lax.ppermute(w_down, "c", swap)

    meta = [routes.astype(half)] + split_weights(route_weights)
    pad = jnp.zeros((micro, local_rows, META - 4 * TOP), half)
    sent = jnp.concatenate([tokens] + meta + [pad], axis=2)
    sent = sent.reshape(micro * local_rows, width + META)
    gathered = lax.all_gather(sent, ("x", "y", "z"), axis=0, tiled=True)

    slot_ids = jnp.arange(slots, dtype=jnp.int32)
    same = slot_expert[:, None] == slot_expert[None, :]
    primary = ~jnp.any(same & (slot_ids[None, :] < slot_ids[:, None]), axis=1)
    held = jnp.where(primary, slot_expert, -1)
    chip = (lax.axis_index("y") * sizes["z"] + lax.axis_index("z")) * 2
    mine = lax.dynamic_slice(held, ((chip + core) * per_device,), (per_device,))
    theirs = lax.dynamic_slice(held, ((chip + 1 - core) * per_device,), (per_device,))
    local = jnp.concatenate([mine, theirs]).astype(jnp.float32)

    down_rows = per_device * w_down.shape[1]
    wide = width // (3 * BLOCK) * BLOCK
    cuts = [0, wide, 2 * wide, width]
    flat_own, flat_other = w_down.reshape(down_rows, width), p_down.reshape(down_rows, width)
    downs = [join(flat_own, flat_other, cuts[c], cuts[c + 1]) for c in range(3)]
    gathered, downs, local = lax.optimization_barrier((gathered, downs, local))

    hidden = gate_up(local, gathered, w_gate, w_up, p_gate, p_up)
    grid = hidden.reshape(
        sizes["x"], sizes["y"], sizes["z"], micro * local_rows, hidden.shape[1]
    )

    def chunk(array, axis, offset, names):
        at = lax.rem(lax.axis_index(axis) + offset + sizes[axis], sizes[axis])
        return lax.dynamic_index_in_dim(array, at, names.index(axis), keepdims=False)

    first = [order[0] for order in ORDERS]
    where = []
    for axis in first:
        place = lax.axis_index(axis) + sizes[axis]
        where.append(jnp.stack([lax.rem(place + n, sizes[axis]) for n in (0, 1, 2, -1)]))
    got = []
    for color, axis in enumerate(first):
        up, down = project(
            grid, downs[color], where[color], "xyz".index(axis), ((2, 1), (3, 2)), half
        )
        got.append((shift(up, axis, 1), shift(down, axis, -1)))
        grid, _, _ = lax.optimization_barrier((grid, up, down))
    kept = [
        project(
            grid, downs[color], where[color], "xyz".index(axis), ((1, 3), (0, 0)), jnp.float32
        )
        for color, axis in enumerate(first)
    ]
    last = []
    for color, axis in enumerate(first):
        middle, _ = kept[color]
        mid = middle.shape[0] // 2
        up, down = got[color]
        near_up = (middle[:mid] + up[:mid].astype(jnp.float32)).astype(half)
        near_down = (middle[mid:] + down[mid:].astype(jnp.float32)).astype(half)
        last.append((shift(near_up, axis, 1), shift(near_down, axis, -1)))
    sums = []
    for color, axis in enumerate(first):
        _, own = kept[color]
        mid = own.shape[0] // 2
        up, down = [v.astype(jnp.float32) for v in got[color]]
        up2, down2 = [v.astype(jnp.float32) for v in last[color]]
        sums.append(
            jnp.concatenate([own[:mid] + up2 + down[:mid], own[mid:] + up[mid:] + down2])
        )
    names = ["xyz".replace(axis, "") for axis in first]
    for stage in (1, 2):
        going, arrived = [], []
        for color in range(3):
            axis = ORDERS[color][stage]
            pieces = [
                chunk(sums[color], axis, offset, names[color]).astype(half)
                for offset in (1, -1, 2)
            ]
            going.append(pieces)
            arrived.append([shift(v, axis, n) for v, n in zip(pieces, (1, -1, 2))])
        sums, _ = lax.optimization_barrier((sums, going))
        for color in range(3):
            axis = ORDERS[color][stage]
            total = chunk(sums[color], axis, 0, names[color])
            for piece in arrived[color]:
                total = total + piece.astype(jnp.float32)
            sums[color] = total
            names[color] = names[color].replace(axis, "")
    result = jnp.concatenate([v.astype(half) for v in sums], axis=1)
    return result.reshape(micro, local_rows, width)


def solution(mesh):
    fine = Mesh(mesh.devices.reshape(4, 4, 4, 2), ("x", "y", "z", "c"))
    row = P(None, ("x", "y", "z", "c"), None)
    column = P(("y", "z", "c"), None, "x")
    in_specs = (row, row, row, P(), column, column, P(("y", "z", "c"), "x", None))
    return jax.shard_map(body, mesh=fine, in_specs=in_specs, out_specs=row, check_vma=False)
```

```python
import functools

import jax
import jax.numpy as jnp
from jax import lax
from jax.experimental import pallas as pl
from jax.experimental.pallas import tpu as pltpu
from jax.sharding import Mesh, PartitionSpec as P


META = 128
TK = 1024
TOP = 8
GROUP = 8
CAP = 2
BLOCK = 256
SEATS = BLOCK // GROUP * CAP
ORDERS = (("z", "y", "x"), ("y", "x", "z"), ("x", "z", "y"))


def gate_up_kernel(
    local_ref, x_ref, meta_ref, wg_ref, wu_ref, pg_ref, pu_ref, h_ref, acc, packed, select, scale
):
    k = pl.program_id(0)
    rows, _ = x_ref.shape
    hid = wg_ref.shape[2]
    blocks = rows // BLOCK
    top = TOP

    @pl.when(k == 0)
    def _():
        acc[...] = jnp.zeros_like(acc)
        early = lax.broadcasted_iota(jnp.int32, (BLOCK, BLOCK), 0)
        late = lax.broadcasted_iota(jnp.int32, (BLOCK, BLOCK), 1)
        before = ((early < late) & (early // GROUP == late // GROUP)).astype(jnp.bfloat16)
        place = lax.broadcasted_iota(jnp.int32, (SEATS, BLOCK), 0).astype(jnp.float32)
        group = lax.broadcasted_iota(jnp.int32, (1, BLOCK), 1) // GROUP
        seat0 = (group * CAP).astype(jnp.float32)
        for b in range(blocks):
            info = meta_ref[b * BLOCK : (b + 1) * BLOCK, :].astype(jnp.float32).T
            chosen = info[:top]
            weight = info[top : 2 * top] + info[2 * top : 3 * top] + info[3 * top : 4 * top]
            for j in range(4):
                hit = chosen == local_ref[j]
                coef = jnp.sum(jnp.where(hit, weight, 0.0), axis=0, keepdims=True)
                active = jnp.sum(jnp.where(hit, 1.0, 0.0), axis=0, keepdims=True)
                earlier = jnp.dot(
                    jnp.broadcast_to(active, (8, BLOCK)).astype(jnp.bfloat16),
                    before,
                    preferred_element_type=jnp.float32,
                )[:1]
                seat = jnp.where(active > 0.5, seat0 + earlier, -1.0)
                taken = place == seat
                select[b, j * SEATS : (j + 1) * SEATS, :] = jnp.where(taken, 1.0, 0.0).astype(
                    jnp.bfloat16
                )
                picked = jnp.sum(jnp.where(taken, coef, 0.0), axis=1, keepdims=True)
                scale[j, b * SEATS : (b + 1) * SEATS, :] = jnp.broadcast_to(picked, (SEATS, 128))

    for b in range(blocks):
        got = jnp.dot(
            select[b], x_ref[b * BLOCK : (b + 1) * BLOCK, :], preferred_element_type=jnp.float32
        ).astype(jnp.bfloat16)
        for j in range(4):
            packed[j, b * SEATS : (b + 1) * SEATS, :] = got[j * SEATS : (j + 1) * SEATS]
    for j in range(4):
        gate_w, up_w = ((wg_ref, wu_ref), (pg_ref, pu_ref))[j // 2]
        x = packed[j]
        acc[j, 0] += jnp.dot(x, gate_w[j % 2], preferred_element_type=jnp.float32)
        acc[j, 1] += jnp.dot(x, up_w[j % 2], preferred_element_type=jnp.float32)

    @pl.when(k == pl.num_programs(0) - 1)
    def _():
        for j in range(4):
            value = jax.nn.silu(acc[j, 0]) * acc[j, 1] * scale[j, :, :1]
            value = value.astype(jnp.bfloat16)
            for b in range(blocks):
                spread = select[b, j * SEATS : (j + 1) * SEATS, :].astype(jnp.float32).T
                h_ref[b * BLOCK : (b + 1) * BLOCK, j * hid : (j + 1) * hid] = jnp.dot(
                    spread.astype(jnp.bfloat16),
                    value[b * SEATS : (b + 1) * SEATS],
                    preferred_element_type=jnp.float32,
                ).astype(jnp.bfloat16)


def gate_up(local, x, wg, wu, pg, pu):
    rows = x.shape[0]
    depth, hid = wg.shape[1], wg.shape[2]
    packed_rows = rows // BLOCK * SEATS
    wspec = pl.BlockSpec((2, TK, hid), lambda k: (0, k, 0))
    return pl.pallas_call(
        gate_up_kernel,
        grid=(depth // TK,),
        in_specs=[
            pl.BlockSpec(memory_space=pltpu.SMEM),
            pl.BlockSpec((rows, TK), lambda k: (0, k)),
            pl.BlockSpec((rows, META), lambda k: (0, depth // META)),
            wspec,
            wspec,
            wspec,
            wspec,
        ],
        out_specs=pl.BlockSpec((rows, 4 * hid), lambda k: (0, 0)),
        out_shape=jax.ShapeDtypeStruct((rows, 4 * hid), jnp.bfloat16),
        scratch_shapes=[
            pltpu.VMEM((4, 2, packed_rows, hid), jnp.float32),
            pltpu.VMEM((4, packed_rows, TK), jnp.bfloat16),
            pltpu.VMEM((rows // BLOCK, 4 * SEATS, BLOCK), jnp.bfloat16),
            pltpu.VMEM((4, packed_rows, 128), jnp.float32),
        ],
        compiler_params=pltpu.CompilerParams(
            dimension_semantics=("arbitrary",), vmem_limit_bytes=60 * 1024 * 1024
        ),
        cost_estimate=pl.CostEstimate(
            flops=2 * packed_rows * depth * 8 * hid,
            bytes_accessed=2 * (rows * depth + 8 * depth * hid),
            transcendentals=packed_rows * 4 * hid,
        ),
    )(local, x, x, wg, wu, pg, pu)


def join_kernel(own_ref, other_ref, out_ref):
    rows = own_ref.shape[0]
    out_ref[:rows] = own_ref[...]
    out_ref[rows:] = other_ref[...]


def join(own, other, lower, upper):
    rows = own.shape[0]
    first = lower // 128
    source = pl.BlockSpec((rows, 128), lambda n: (0, first + n))
    return pl.pallas_call(
        join_kernel,
        grid=((upper - lower) // 128,),
        in_specs=[source, source],
        out_specs=pl.BlockSpec((2 * rows, 128), lambda n: (0, n)),
        out_shape=jax.ShapeDtypeStruct((2 * rows, upper - lower), own.dtype),
        cost_estimate=pl.CostEstimate(
            flops=0, bytes_accessed=8 * rows * (upper - lower), transcendentals=0
        ),
    )(own, other)


def project_kernel(dim, picks, at_ref, h_ref, w_ref, *refs):
    outs, rows_ref = refs[:-1], refs[-1]
    lead = h_ref.shape[0] // 2

    @pl.when(pl.program_id(0) == 0)
    def _():
        start = 0
        for pair in picks:
            for side, pick in enumerate(pair):
                at = at_ref[pick]
                lo = side * lead
                if dim == 0:
                    part = h_ref[at, lo : lo + lead]
                elif dim == 1:
                    part = h_ref[lo : lo + lead, at]
                else:
                    part = h_ref[lo : lo + lead, :, at]
                part = part.reshape(-1, h_ref.shape[-1])
                rows_ref[start : start + part.shape[0]] = part
                start += part.shape[0]

    count = rows_ref.shape[0] // len(outs)
    for n, out in enumerate(outs):
        value = jnp.dot(
            rows_ref[n * count : (n + 1) * count], w_ref[...], preferred_element_type=jnp.float32
        )
        out[...] = value.astype(out.dtype).reshape(out.shape)


def project(grid, weights, at, dim, picks, dtype):
    depth = grid.shape[-1]
    rest = [n for i, n in enumerate(grid.shape[:3]) if i != dim] + [grid.shape[3]]
    columns = weights.shape[1]
    rows = rest[0] * rest[1] * rest[2]
    tile = columns // 3 if columns % 384 == 0 else columns // 4
    return pl.pallas_call(
        functools.partial(project_kernel, dim, picks),
        grid=(columns // tile,),
        in_specs=[
            pl.BlockSpec(memory_space=pltpu.SMEM),
            pl.BlockSpec(grid.shape, lambda n: (0, 0, 0, 0, 0)),
            pl.BlockSpec((depth, tile), lambda n: (0, n)),
        ],
        out_specs=[pl.BlockSpec((*rest, tile), lambda n: (0, 0, 0, n))] * len(picks),
        out_shape=[jax.ShapeDtypeStruct((*rest, columns), dtype)] * len(picks),
        scratch_shapes=[pltpu.VMEM((rows * len(picks), depth), jnp.bfloat16)],
        compiler_params=pltpu.CompilerParams(
            dimension_semantics=("arbitrary",), vmem_limit_bytes=60 * 1024 * 1024
        ),
        cost_estimate=pl.CostEstimate(
            flops=2 * rows * len(picks) * depth * columns,
            bytes_accessed=2 * depth * columns,
            transcendentals=0,
        ),
    )(at, grid, weights)


def shift(value, axis, by):
    size = lax.axis_size(axis)
    return lax.ppermute(value, axis, [(i, (i + by) % size) for i in range(size)])


def split_weights(w):
    hi = lax.reduce_precision(w, 8, 7)
    mid = lax.reduce_precision(w - hi, 8, 7)
    lo = lax.reduce_precision(w - hi - mid, 8, 7)
    return [v.astype(jnp.bfloat16) for v in (hi, mid, lo)]


def body(tokens, routes, route_weights, slot_expert, w_gate, w_up, w_down):
    micro, local_rows, width = tokens.shape
    slots = slot_expert.shape[0]
    per_device = w_gate.shape[0]
    core = lax.axis_index("c")
    sizes = {a: lax.axis_size(a) for a in "xyz"}
    half = jnp.bfloat16

    swap = [(0, 1), (1, 0)]
    p_gate = lax.ppermute(w_gate, "c", swap)
    p_up = lax.ppermute(w_up, "c", swap)
    p_down = lax.ppermute(w_down, "c", swap)

    meta = [routes.astype(half)] + split_weights(route_weights)
    pad = jnp.zeros((micro, local_rows, META - 4 * TOP), half)
    sent = jnp.concatenate([tokens] + meta + [pad], axis=2)
    sent = sent.reshape(micro * local_rows, width + META)
    gathered = lax.all_gather(sent, ("x", "y", "z"), axis=0, tiled=True)

    slot_ids = jnp.arange(slots, dtype=jnp.int32)
    same = slot_expert[:, None] == slot_expert[None, :]
    primary = ~jnp.any(same & (slot_ids[None, :] < slot_ids[:, None]), axis=1)
    held = jnp.where(primary, slot_expert, -1)
    chip = (lax.axis_index("y") * sizes["z"] + lax.axis_index("z")) * 2
    mine = lax.dynamic_slice(held, ((chip + core) * per_device,), (per_device,))
    theirs = lax.dynamic_slice(held, ((chip + 1 - core) * per_device,), (per_device,))
    local = jnp.concatenate([mine, theirs]).astype(jnp.float32)

    down_rows = per_device * w_down.shape[1]
    wide = width // (3 * BLOCK) * BLOCK
    cuts = [0, wide, 2 * wide, width]
    flat_own, flat_other = w_down.reshape(down_rows, width), p_down.reshape(down_rows, width)
    downs = [join(flat_own, flat_other, cuts[c], cuts[c + 1]) for c in range(3)]
    gathered, downs, local = lax.optimization_barrier((gathered, downs, local))

    hidden = gate_up(local, gathered, w_gate, w_up, p_gate, p_up)
    grid = hidden.reshape(
        sizes["x"], sizes["y"], sizes["z"], micro * local_rows, hidden.shape[1]
    )

    def chunk(array, axis, offset, names):
        at = lax.rem(lax.axis_index(axis) + offset + sizes[axis], sizes[axis])
        return lax.dynamic_index_in_dim(array, at, names.index(axis), keepdims=False)

    first = [order[0] for order in ORDERS]
    where = []
    for axis in first:
        place = lax.axis_index(axis) + sizes[axis]
        where.append(jnp.stack([lax.rem(place + n, sizes[axis]) for n in (0, 1, 2, -1)]))
    got = []
    for color, axis in enumerate(first):
        up, down = project(
            grid, downs[color], where[color], "xyz".index(axis), ((2, 1), (3, 2)), half
        )
        far_up = shift(up, axis, 1)
        far_down = shift(down, axis, -1)
        got.append((far_up, far_down))
        grid, _, _ = lax.optimization_barrier((grid, up, down))
    kept = []
    for color, axis in enumerate(first):
        kept.append(
            project(
                grid,
                downs[color],
                where[color],
                "xyz".index(axis),
                ((1, 3), (0, 0)),
                jnp.float32,
            )
        )
    last = []
    for color, axis in enumerate(first):
        middle, _ = kept[color]
        mid = middle.shape[0] // 2
        up, down = got[color]
        near_up = (middle[:mid] + up[:mid].astype(jnp.float32)).astype(half)
        near_down = (middle[mid:] + down[mid:].astype(jnp.float32)).astype(half)
        last.append((shift(near_up, axis, 1), shift(near_down, axis, -1)))
    sums = []
    for color, axis in enumerate(first):
        _, own = kept[color]
        mid = own.shape[0] // 2
        up, down = [v.astype(jnp.float32) for v in got[color]]
        up2, down2 = [v.astype(jnp.float32) for v in last[color]]
        sums.append(
            jnp.concatenate([own[:mid] + up2 + down[:mid], own[mid:] + up[mid:] + down2])
        )
    names = ["xyz".replace(axis, "") for axis in first]
    for stage in (1, 2):
        going, arrived = [], []
        for color in range(3):
            axis = ORDERS[color][stage]
            pieces = [
                chunk(sums[color], axis, offset, names[color]).astype(half)
                for offset in (1, -1, 2)
            ]
            going.append(pieces)
            arrived.append([shift(v, axis, n) for v, n in zip(pieces, (1, -1, 2))])
        sums, _ = lax.optimization_barrier((sums, going))
        for color in range(3):
            axis = ORDERS[color][stage]
            total = chunk(sums[color], axis, 0, names[color])
            for piece in arrived[color]:
                total = total + piece.astype(jnp.float32)
            sums[color] = total
            names[color] = names[color].replace(axis, "")
    result = jnp.concatenate([v.astype(half) for v in sums], axis=1)
    return result.reshape(micro, local_rows, width)


def solution(mesh):
    fine = Mesh(mesh.devices.reshape(4, 4, 4, 2), ("x", "y", "z", "c"))
    row = P(None, ("x", "y", "z", "c"), None)
    column = P(("y", "z", "c"), None, "x")
    in_specs = (row, row, row, P(), column, column, P(("y", "z", "c"), "x", None))
    return jax.shard_map(body, mesh=fine, in_specs=in_specs, out_specs=row, check_vma=False)
```

```python
import functools

import jax
import jax.numpy as jnp
from jax import lax
from jax.experimental import pallas as pl
from jax.experimental.pallas import tpu as pltpu
from jax.sharding import Mesh, PartitionSpec as P


META = 128
TK = 1024
TOP = 8
GROUP = 8
CAP = 2
BLOCK = 256
SEATS = BLOCK // GROUP * CAP
ORDERS = (("z", "y", "x"), ("y", "x", "z"), ("x", "z", "y"))


def gate_up_kernel(
    local_ref, x_ref, meta_ref, wg_ref, wu_ref, pg_ref, pu_ref, h_ref, acc, packed, select, scale
):
    k = pl.program_id(0)
    rows, _ = x_ref.shape
    hid = wg_ref.shape[2]
    blocks = rows // BLOCK
    top = TOP

    @pl.when(k == 0)
    def _():
        acc[...] = jnp.zeros_like(acc)
        early = lax.broadcasted_iota(jnp.int32, (BLOCK, BLOCK), 0)
        late = lax.broadcasted_iota(jnp.int32, (BLOCK, BLOCK), 1)
        before = ((early < late) & (early // GROUP == late // GROUP)).astype(jnp.bfloat16)
        place = lax.broadcasted_iota(jnp.int32, (SEATS, BLOCK), 0).astype(jnp.float32)
        group = lax.broadcasted_iota(jnp.int32, (1, BLOCK), 1) // GROUP
        seat0 = (group * CAP).astype(jnp.float32)
        for b in range(blocks):
            info = meta_ref[b * BLOCK : (b + 1) * BLOCK, :].astype(jnp.float32).T
            chosen = info[:top]
            weight = info[top : 2 * top] + info[2 * top : 3 * top] + info[3 * top : 4 * top]
            for j in range(4):
                hit = chosen == local_ref[j]
                coef = jnp.sum(jnp.where(hit, weight, 0.0), axis=0, keepdims=True)
                active = jnp.sum(jnp.where(hit, 1.0, 0.0), axis=0, keepdims=True)
                earlier = jnp.dot(
                    jnp.broadcast_to(active, (8, BLOCK)).astype(jnp.bfloat16),
                    before,
                    preferred_element_type=jnp.float32,
                )[:1]
                seat = jnp.where(active > 0.5, seat0 + earlier, -1.0)
                taken = place == seat
                select[b, j * SEATS : (j + 1) * SEATS, :] = jnp.where(taken, 1.0, 0.0).astype(
                    jnp.bfloat16
                )
                picked = jnp.sum(jnp.where(taken, coef, 0.0), axis=1, keepdims=True)
                scale[j, b * SEATS : (b + 1) * SEATS, :] = jnp.broadcast_to(picked, (SEATS, 128))

    for b in range(blocks):
        got = jnp.dot(
            select[b], x_ref[b * BLOCK : (b + 1) * BLOCK, :], preferred_element_type=jnp.float32
        ).astype(jnp.bfloat16)
        for j in range(4):
            packed[j, b * SEATS : (b + 1) * SEATS, :] = got[j * SEATS : (j + 1) * SEATS]
    for j in range(4):
        gate_w, up_w = ((wg_ref, wu_ref), (pg_ref, pu_ref))[j // 2]
        x = packed[j]
        acc[j, 0] += jnp.dot(x, gate_w[j % 2], preferred_element_type=jnp.float32)
        acc[j, 1] += jnp.dot(x, up_w[j % 2], preferred_element_type=jnp.float32)

    @pl.when(k == pl.num_programs(0) - 1)
    def _():
        for j in range(4):
            value = jax.nn.silu(acc[j, 0]) * acc[j, 1] * scale[j, :, :1]
            value = value.astype(jnp.bfloat16)
            for b in range(blocks):
                spread = select[b, j * SEATS : (j + 1) * SEATS, :].astype(jnp.float32).T
                h_ref[b * BLOCK : (b + 1) * BLOCK, j * hid : (j + 1) * hid] = jnp.dot(
                    spread.astype(jnp.bfloat16),
                    value[b * SEATS : (b + 1) * SEATS],
                    preferred_element_type=jnp.float32,
                ).astype(jnp.bfloat16)


def gate_up(local, x, wg, wu, pg, pu):
    rows = x.shape[0]
    depth, hid = wg.shape[1], wg.shape[2]
    packed_rows = rows // BLOCK * SEATS
    wspec = pl.BlockSpec((2, TK, hid), lambda k: (0, k, 0))
    return pl.pallas_call(
        gate_up_kernel,
        grid=(depth // TK,),
        in_specs=[
            pl.BlockSpec(memory_space=pltpu.SMEM),
            pl.BlockSpec((rows, TK), lambda k: (0, k)),
            pl.BlockSpec((rows, META), lambda k: (0, depth // META)),
            wspec,
            wspec,
            wspec,
            wspec,
        ],
        out_specs=pl.BlockSpec((rows, 4 * hid), lambda k: (0, 0)),
        out_shape=jax.ShapeDtypeStruct((rows, 4 * hid), jnp.bfloat16),
        scratch_shapes=[
            pltpu.VMEM((4, 2, packed_rows, hid), jnp.float32),
            pltpu.VMEM((4, packed_rows, TK), jnp.bfloat16),
            pltpu.VMEM((rows // BLOCK, 4 * SEATS, BLOCK), jnp.bfloat16),
            pltpu.VMEM((4, packed_rows, 128), jnp.float32),
        ],
        compiler_params=pltpu.CompilerParams(
            dimension_semantics=("arbitrary",), vmem_limit_bytes=60 * 1024 * 1024
        ),
        cost_estimate=pl.CostEstimate(
            flops=2 * packed_rows * depth * 8 * hid,
            bytes_accessed=2 * (rows * depth + 8 * depth * hid),
            transcendentals=packed_rows * 4 * hid,
        ),
    )(local, x, x, wg, wu, pg, pu)


def join_kernel(own_ref, other_ref, out_ref):
    rows = own_ref.shape[0]
    out_ref[:rows] = own_ref[...]
    out_ref[rows:] = other_ref[...]


def join(own, other, lower, upper):
    rows = own.shape[0]
    first = lower // 128
    source = pl.BlockSpec((rows, 128), lambda n: (0, first + n))
    return pl.pallas_call(
        join_kernel,
        grid=((upper - lower) // 128,),
        in_specs=[source, source],
        out_specs=pl.BlockSpec((2 * rows, 128), lambda n: (0, n)),
        out_shape=jax.ShapeDtypeStruct((2 * rows, upper - lower), own.dtype),
        cost_estimate=pl.CostEstimate(
            flops=0, bytes_accessed=8 * rows * (upper - lower), transcendentals=0
        ),
    )(own, other)


def project_kernel(dim, picks, at_ref, h_ref, w_ref, *refs):
    outs, rows_ref = refs[:-1], refs[-1]
    lead = h_ref.shape[0] // 2

    @pl.when(pl.program_id(0) == 0)
    def _():
        start = 0
        for pair in picks:
            for side, pick in enumerate(pair):
                at = at_ref[pick]
                lo = side * lead
                if dim == 0:
                    part = h_ref[at, lo : lo + lead]
                elif dim == 1:
                    part = h_ref[lo : lo + lead, at]
                else:
                    part = h_ref[lo : lo + lead, :, at]
                part = part.reshape(-1, h_ref.shape[-1])
                rows_ref[start : start + part.shape[0]] = part
                start += part.shape[0]

    count = rows_ref.shape[0] // len(outs)
    for n, out in enumerate(outs):
        value = jnp.dot(
            rows_ref[n * count : (n + 1) * count], w_ref[...], preferred_element_type=jnp.float32
        )
        out[...] = value.astype(out.dtype).reshape(out.shape)


def project_late(grid, weights, at, dim, picks, dtype):
    size, depth = grid.shape[0], grid.shape[-1]
    rest = [n for i, n in enumerate(grid.shape[:3]) if i != dim] + [grid.shape[3]]
    columns = weights.shape[1]
    rows = rest[0] * rest[1] * rest[2]
    tile = columns // 3 if columns % 384 == 0 else columns // 4
    return pl.pallas_call(
        functools.partial(project_kernel, dim, picks),
        grid=(columns // tile,),
        in_specs=[
            pl.BlockSpec(memory_space=pltpu.SMEM),
            pl.BlockSpec(grid.shape, lambda n: (0, 0, 0, 0, 0)),
            pl.BlockSpec((depth, tile), lambda n: (0, n)),
        ],
        out_specs=[pl.BlockSpec((*rest, tile), lambda n: (0, 0, 0, n))] * len(picks),
        out_shape=[jax.ShapeDtypeStruct((*rest, columns), dtype)] * len(picks),
        scratch_shapes=[pltpu.VMEM((rows * len(picks), depth), jnp.bfloat16)],
        compiler_params=pltpu.CompilerParams(
            dimension_semantics=("arbitrary",), vmem_limit_bytes=60 * 1024 * 1024
        ),
        cost_estimate=pl.CostEstimate(
            flops=2 * rows * len(picks) * depth * columns,
            bytes_accessed=2 * depth * columns,
            transcendentals=0,
        ),
    )(at, grid, weights)


def shift(value, axis, by):
    size = lax.axis_size(axis)
    return lax.ppermute(value, axis, [(i, (i + by) % size) for i in range(size)])


def split_weights(w):
    hi = lax.reduce_precision(w, 8, 7)
    mid = lax.reduce_precision(w - hi, 8, 7)
    lo = lax.reduce_precision(w - hi - mid, 8, 7)
    return [v.astype(jnp.bfloat16) for v in (hi, mid, lo)]


def body(tokens, routes, route_weights, slot_expert, w_gate, w_up, w_down):
    micro, local_rows, width = tokens.shape
    slots = slot_expert.shape[0]
    per_device = w_gate.shape[0]
    core = lax.axis_index("c")
    sizes = {a: lax.axis_size(a) for a in "xyz"}
    half = jnp.bfloat16

    swap = [(0, 1), (1, 0)]
    p_gate = lax.ppermute(w_gate, "c", swap)
    p_up = lax.ppermute(w_up, "c", swap)
    p_down = lax.ppermute(w_down, "c", swap)

    meta = [routes.astype(half)] + split_weights(route_weights)
    pad = jnp.zeros((micro, local_rows, META - 4 * TOP), half)
    sent = jnp.concatenate([tokens] + meta + [pad], axis=2)
    sent = sent.reshape(micro * local_rows, width + META)
    gathered = lax.all_gather(sent, ("x", "y", "z"), axis=0, tiled=True)

    slot_ids = jnp.arange(slots, dtype=jnp.int32)
    same = slot_expert[:, None] == slot_expert[None, :]
    primary = ~jnp.any(same & (slot_ids[None, :] < slot_ids[:, None]), axis=1)
    held = jnp.where(primary, slot_expert, -1)
    chip = (lax.axis_index("y") * sizes["z"] + lax.axis_index("z")) * 2
    mine = lax.dynamic_slice(held, ((chip + core) * per_device,), (per_device,))
    theirs = lax.dynamic_slice(held, ((chip + 1 - core) * per_device,), (per_device,))
    local = jnp.concatenate([mine, theirs]).astype(jnp.float32)

    down_rows = per_device * w_down.shape[1]
    wide = width // (3 * BLOCK) * BLOCK
    cuts = [0, wide, 2 * wide, width]
    flat_own, flat_other = w_down.reshape(down_rows, width), p_down.reshape(down_rows, width)
    downs = [join(flat_own, flat_other, cuts[c], cuts[c + 1]) for c in range(3)]
    gathered, downs, local = lax.optimization_barrier((gathered, downs, local))

    hidden = gate_up(local, gathered, w_gate, w_up, p_gate, p_up)
    grid = hidden.reshape(
        sizes["x"], sizes["y"], sizes["z"], micro * local_rows, hidden.shape[1]
    )

    def chunk(array, axis, offset, names):
        at = lax.rem(lax.axis_index(axis) + offset + sizes[axis], sizes[axis])
        return lax.dynamic_index_in_dim(array, at, names.index(axis), keepdims=False)

    def project(color, parts):
        part = jnp.concatenate(parts)
        value = jnp.dot(
            part.reshape(-1, part.shape[-1]), downs[color], preferred_element_type=jnp.float32
        )
        return value.reshape(part.shape[:-1] + (value.shape[-1],))

    first = [order[0] for order in ORDERS]
    mid = grid.shape[0] // 2
    got = []
    for color, axis in enumerate(first):
        far = chunk(grid, axis, 2, "xyz")
        up = project(color, [far[:mid], chunk(grid, axis, 1, "xyz")[mid:]]).astype(half)
        down = project(color, [chunk(grid, axis, -1, "xyz")[:mid], far[mid:]]).astype(half)
        got.append((shift(up, axis, 1), shift(down, axis, -1)))
        grid, _, _ = lax.optimization_barrier((grid, up, down))
    kept = []
    for color, axis in enumerate(first):
        place = lax.axis_index(axis) + sizes[axis]
        where = jnp.stack([lax.rem(place + n, sizes[axis]) for n in (0, 1, -1)])
        kept.append(
            project_late(
                grid, downs[color], where, "xyz".index(axis), ((1, 2), (0, 0)), jnp.float32
            )
        )
    last = []
    for color, axis in enumerate(first):
        near, _ = kept[color]
        up, down = got[color]
        near_up = (near[:mid] + up[:mid].astype(jnp.float32)).astype(half)
        near_down = (near[mid:] + down[mid:].astype(jnp.float32)).astype(half)
        last.append((shift(near_up, axis, 1), shift(near_down, axis, -1)))
    sums = []
    for color, axis in enumerate(first):
        _, own = kept[color]
        up, down = [v.astype(jnp.float32) for v in got[color]]
        up2, down2 = [v.astype(jnp.float32) for v in last[color]]
        sums.append(
            jnp.concatenate([own[:mid] + up2 + down[:mid], own[mid:] + up[mid:] + down2])
        )
    names = ["xyz".replace(axis, "") for axis in first]
    for stage in (1, 2):
        going, arrived = [], []
        for color in range(3):
            axis = ORDERS[color][stage]
            pieces = [
                chunk(sums[color], axis, offset, names[color]).astype(half)
                for offset in (1, -1, 2)
            ]
            going.append(pieces)
            arrived.append([shift(v, axis, n) for v, n in zip(pieces, (1, -1, 2))])
        sums, _ = lax.optimization_barrier((sums, going))
        for color in range(3):
            axis = ORDERS[color][stage]
            total = chunk(sums[color], axis, 0, names[color])
            for piece in arrived[color]:
                total = total + piece.astype(jnp.float32)
            sums[color] = total
            names[color] = names[color].replace(axis, "")
    result = jnp.concatenate([v.astype(half) for v in sums], axis=1)
    return result.reshape(micro, local_rows, width)


def solution(mesh):
    fine = Mesh(mesh.devices.reshape(4, 4, 4, 2), ("x", "y", "z", "c"))
    row = P(None, ("x", "y", "z", "c"), None)
    column = P(("y", "z", "c"), None, "x")
    in_specs = (row, row, row, P(), column, column, P(("y", "z", "c"), "x", None))
    return jax.shard_map(body, mesh=fine, in_specs=in_specs, out_specs=row, check_vma=False)
```

```python
import functools

import jax
import jax.numpy as jnp
from jax import lax
from jax.experimental import pallas as pl
from jax.experimental.pallas import tpu as pltpu
from jax.sharding import Mesh, PartitionSpec as P


META = 128
TK = 1024
TOP = 8
GROUP = 8
CAP = 2
BLOCK = 256
SEATS = BLOCK // GROUP * CAP
ORDERS = (("z", "y", "x"), ("y", "x", "z"), ("x", "z", "y"))


def gate_up_kernel(
    local_ref, x_ref, meta_ref, wg_ref, wu_ref, pg_ref, pu_ref, h_ref, acc, packed, select, scale
):
    k = pl.program_id(0)
    rows, _ = x_ref.shape
    hid = wg_ref.shape[2]
    blocks = rows // BLOCK
    top = TOP

    @pl.when(k == 0)
    def _():
        acc[...] = jnp.zeros_like(acc)
        early = lax.broadcasted_iota(jnp.int32, (BLOCK, BLOCK), 0)
        late = lax.broadcasted_iota(jnp.int32, (BLOCK, BLOCK), 1)
        before = ((early < late) & (early // GROUP == late // GROUP)).astype(jnp.bfloat16)
        place = lax.broadcasted_iota(jnp.int32, (SEATS, BLOCK), 0).astype(jnp.float32)
        group = lax.broadcasted_iota(jnp.int32, (1, BLOCK), 1) // GROUP
        seat0 = (group * CAP).astype(jnp.float32)
        for b in range(blocks):
            info = meta_ref[b * BLOCK : (b + 1) * BLOCK, :].astype(jnp.float32).T
            chosen = info[:top]
            weight = info[top : 2 * top] + info[2 * top : 3 * top] + info[3 * top : 4 * top]
            for j in range(4):
                hit = chosen == local_ref[j]
                coef = jnp.sum(jnp.where(hit, weight, 0.0), axis=0, keepdims=True)
                active = jnp.sum(jnp.where(hit, 1.0, 0.0), axis=0, keepdims=True)
                earlier = jnp.dot(
                    jnp.broadcast_to(active, (8, BLOCK)).astype(jnp.bfloat16),
                    before,
                    preferred_element_type=jnp.float32,
                )[:1]
                seat = jnp.where(active > 0.5, seat0 + earlier, -1.0)
                taken = place == seat
                select[b, j * SEATS : (j + 1) * SEATS, :] = jnp.where(taken, 1.0, 0.0).astype(
                    jnp.bfloat16
                )
                picked = jnp.sum(jnp.where(taken, coef, 0.0), axis=1, keepdims=True)
                scale[j, b * SEATS : (b + 1) * SEATS, :] = jnp.broadcast_to(picked, (SEATS, 128))

    for b in range(blocks):
        got = jnp.dot(
            select[b], x_ref[b * BLOCK : (b + 1) * BLOCK, :], preferred_element_type=jnp.float32
        ).astype(jnp.bfloat16)
        for j in range(4):
            packed[j, b * SEATS : (b + 1) * SEATS, :] = got[j * SEATS : (j + 1) * SEATS]
    for j in range(4):
        gate_w, up_w = ((wg_ref, wu_ref), (pg_ref, pu_ref))[j // 2]
        x = packed[j]
        acc[j, 0] += jnp.dot(x, gate_w[j % 2], preferred_element_type=jnp.float32)
        acc[j, 1] += jnp.dot(x, up_w[j % 2], preferred_element_type=jnp.float32)

    @pl.when(k == pl.num_programs(0) - 1)
    def _():
        for j in range(4):
            value = jax.nn.silu(acc[j, 0]) * acc[j, 1] * scale[j, :, :1]
            value = value.astype(jnp.bfloat16)
            for b in range(blocks):
                spread = select[b, j * SEATS : (j + 1) * SEATS, :].astype(jnp.float32).T
                h_ref[b * BLOCK : (b + 1) * BLOCK, j * hid : (j + 1) * hid] = jnp.dot(
                    spread.astype(jnp.bfloat16),
                    value[b * SEATS : (b + 1) * SEATS],
                    preferred_element_type=jnp.float32,
                ).astype(jnp.bfloat16)


def gate_up(local, x, wg, wu, pg, pu):
    rows = x.shape[0]
    depth, hid = wg.shape[1], wg.shape[2]
    packed_rows = rows // BLOCK * SEATS
    wspec = pl.BlockSpec((2, TK, hid), lambda k: (0, k, 0))
    return pl.pallas_call(
        gate_up_kernel,
        grid=(depth // TK,),
        in_specs=[
            pl.BlockSpec(memory_space=pltpu.SMEM),
            pl.BlockSpec((rows, TK), lambda k: (0, k)),
            pl.BlockSpec((rows, META), lambda k: (0, depth // META)),
            wspec,
            wspec,
            wspec,
            wspec,
        ],
        out_specs=pl.BlockSpec((rows, 4 * hid), lambda k: (0, 0)),
        out_shape=jax.ShapeDtypeStruct((rows, 4 * hid), jnp.bfloat16),
        scratch_shapes=[
            pltpu.VMEM((4, 2, packed_rows, hid), jnp.float32),
            pltpu.VMEM((4, packed_rows, TK), jnp.bfloat16),
            pltpu.VMEM((rows // BLOCK, 4 * SEATS, BLOCK), jnp.bfloat16),
            pltpu.VMEM((4, packed_rows, 128), jnp.float32),
        ],
        compiler_params=pltpu.CompilerParams(
            dimension_semantics=("arbitrary",), vmem_limit_bytes=58 * 1024 * 1024
        ),
        cost_estimate=pl.CostEstimate(
            flops=2 * packed_rows * depth * 8 * hid,
            bytes_accessed=2 * (rows * depth + 8 * depth * hid),
            transcendentals=packed_rows * 4 * hid,
        ),
    )(local, x, x, wg, wu, pg, pu)


def join_kernel(own_ref, other_ref, out_ref):
    rows = own_ref.shape[0]
    out_ref[:rows] = own_ref[...]
    out_ref[rows:] = other_ref[...]


def join(own, other, lower, upper):
    rows = own.shape[0]
    first = lower // 128
    source = pl.BlockSpec((rows, 128), lambda n: (0, first + n))
    return pl.pallas_call(
        join_kernel,
        grid=((upper - lower) // 128,),
        in_specs=[source, source],
        out_specs=pl.BlockSpec((2 * rows, 128), lambda n: (0, n)),
        out_shape=jax.ShapeDtypeStruct((2 * rows, upper - lower), own.dtype),
        cost_estimate=pl.CostEstimate(
            flops=0, bytes_accessed=8 * rows * (upper - lower), transcendentals=0
        ),
    )(own, other)


def project_kernel(dim, picks, at_ref, h_ref, w_ref, *refs):
    outs, rows_ref = refs[:-1], refs[-1]
    lead = h_ref.shape[0] // 2

    @pl.when(pl.program_id(0) == 0)
    def _():
        start = 0
        for pair in picks:
            for side, pick in enumerate(pair):
                at = at_ref[pick]
                lo = side * lead
                if dim == 0:
                    part = h_ref[at, lo : lo + lead]
                elif dim == 1:
                    part = h_ref[lo : lo + lead, at]
                else:
                    part = h_ref[lo : lo + lead, :, at]
                part = part.reshape(-1, h_ref.shape[-1])
                rows_ref[start : start + part.shape[0]] = part
                start += part.shape[0]

    count = rows_ref.shape[0] // len(outs)
    for n, out in enumerate(outs):
        value = jnp.dot(
            rows_ref[n * count : (n + 1) * count], w_ref[...], preferred_element_type=jnp.float32
        )
        out[...] = value.astype(out.dtype).reshape(out.shape)


def project_late(grid, weights, at, dim, picks, dtype):
    depth = grid.shape[-1]
    rest = [n for i, n in enumerate(grid.shape[:3]) if i != dim] + [grid.shape[3]]
    columns = weights.shape[1]
    rows = rest[0] * rest[1] * rest[2]
    tile = columns // 3 if columns % 384 == 0 else columns // 4
    return pl.pallas_call(
        functools.partial(project_kernel, dim, picks),
        grid=(columns // tile,),
        in_specs=[
            pl.BlockSpec(memory_space=pltpu.SMEM),
            pl.BlockSpec(grid.shape, lambda n: (0, 0, 0, 0, 0)),
            pl.BlockSpec((depth, tile), lambda n: (0, n)),
        ],
        out_specs=[pl.BlockSpec((*rest, tile), lambda n: (0, 0, 0, n))] * len(picks),
        out_shape=[jax.ShapeDtypeStruct((*rest, columns), dtype)] * len(picks),
        scratch_shapes=[pltpu.VMEM((rows * len(picks), depth), jnp.bfloat16)],
        compiler_params=pltpu.CompilerParams(
            dimension_semantics=("arbitrary",), vmem_limit_bytes=60 * 1024 * 1024
        ),
        cost_estimate=pl.CostEstimate(
            flops=2 * rows * len(picks) * depth * columns,
            bytes_accessed=2 * depth * columns,
            transcendentals=0,
        ),
    )(at, grid, weights)


def shift(value, axis, by):
    size = lax.axis_size(axis)
    return lax.ppermute(value, axis, [(i, (i + by) % size) for i in range(size)])


def split_weights(w):
    hi = lax.reduce_precision(w, 8, 7)
    mid = lax.reduce_precision(w - hi, 8, 7)
    lo = lax.reduce_precision(w - hi - mid, 8, 7)
    return [v.astype(jnp.bfloat16) for v in (hi, mid, lo)]


def body(tokens, routes, route_weights, slot_expert, w_gate, w_up, w_down):
    micro, local_rows, width = tokens.shape
    slots = slot_expert.shape[0]
    per_device = w_gate.shape[0]
    core = lax.axis_index("c")
    sizes = {a: lax.axis_size(a) for a in "xyz"}
    half = jnp.bfloat16

    swap = [(0, 1), (1, 0)]
    p_gate = lax.ppermute(w_gate, "c", swap)
    p_up = lax.ppermute(w_up, "c", swap)
    p_down = lax.ppermute(w_down, "c", swap)

    meta = [routes.astype(half)] + split_weights(route_weights)
    pad = jnp.zeros((micro, local_rows, META - 4 * TOP), half)
    sent = jnp.concatenate([tokens] + meta + [pad], axis=2)
    sent = sent.reshape(micro * local_rows, width + META)
    gathered = lax.all_gather(sent, ("x", "y", "z"), axis=0, tiled=True)

    slot_ids = jnp.arange(slots, dtype=jnp.int32)
    same = slot_expert[:, None] == slot_expert[None, :]
    primary = ~jnp.any(same & (slot_ids[None, :] < slot_ids[:, None]), axis=1)
    held = jnp.where(primary, slot_expert, -1)
    chip = (lax.axis_index("y") * sizes["z"] + lax.axis_index("z")) * 2
    mine = lax.dynamic_slice(held, ((chip + core) * per_device,), (per_device,))
    theirs = lax.dynamic_slice(held, ((chip + 1 - core) * per_device,), (per_device,))
    local = jnp.concatenate([mine, theirs]).astype(jnp.float32)

    down_rows = per_device * w_down.shape[1]
    wide = width // (3 * BLOCK) * BLOCK
    cuts = [0, wide, 2 * wide, width]
    flat_own, flat_other = w_down.reshape(down_rows, width), p_down.reshape(down_rows, width)
    downs = [join(flat_own, flat_other, cuts[c], cuts[c + 1]) for c in range(3)]
    gathered, downs, local = lax.optimization_barrier((gathered, downs, local))

    hidden = gate_up(local, gathered, w_gate, w_up, p_gate, p_up)
    grid = hidden.reshape(
        sizes["x"], sizes["y"], sizes["z"], micro * local_rows, hidden.shape[1]
    )

    def chunk(array, axis, offset, names):
        at = lax.rem(lax.axis_index(axis) + offset + sizes[axis], sizes[axis])
        return lax.dynamic_index_in_dim(array, at, names.index(axis), keepdims=False)

    def project(color, parts):
        part = jnp.concatenate(parts)
        value = jnp.dot(
            part.reshape(-1, part.shape[-1]), downs[color], preferred_element_type=jnp.float32
        )
        return value.reshape(part.shape[:-1] + (value.shape[-1],))

    first = [order[0] for order in ORDERS]
    mid = grid.shape[0] // 2
    got = []
    for color, axis in enumerate(first):
        far = chunk(grid, axis, 2, "xyz")
        up = project(color, [far[:mid], chunk(grid, axis, 1, "xyz")[mid:]]).astype(half)
        down = project(color, [chunk(grid, axis, -1, "xyz")[:mid], far[mid:]]).astype(half)
        got.append((shift(up, axis, 1), shift(down, axis, -1)))
        grid, _, _ = lax.optimization_barrier((grid, up, down))
    where, nears = [], []
    for color, axis in enumerate(first):
        place = lax.axis_index(axis) + sizes[axis]
        where.append(jnp.stack([lax.rem(place + n, sizes[axis]) for n in (0, 1, -1)]))
        (near,) = project_late(
            grid, downs[color], where[color], "xyz".index(axis), ((1, 2),), jnp.float32
        )
        nears.append(near)
    last = []
    for color, axis in enumerate(first):
        near = nears[color]
        up, down = got[color]
        near_up = (near[:mid] + up[:mid].astype(jnp.float32)).astype(half)
        near_down = (near[mid:] + down[mid:].astype(jnp.float32)).astype(half)
        last_up = shift(near_up, axis, 1)
        last_down = shift(near_down, axis, -1)
        last.append((last_up, last_down))
    sums = []
    for color, axis in enumerate(first):
        (own,) = project_late(
            grid, downs[color], where[color], "xyz".index(axis), ((0, 0),), jnp.float32
        )
        up, down = [v.astype(jnp.float32) for v in got[color]]
        up2, down2 = [v.astype(jnp.float32) for v in last[color]]
        sums.append(
            jnp.concatenate([own[:mid] + up2 + down[:mid], own[mid:] + up[mid:] + down2])
        )
    names = ["xyz".replace(axis, "") for axis in first]
    for stage in (1, 2):
        going, arrived = [], []
        for color in range(3):
            axis = ORDERS[color][stage]
            pieces = [
                chunk(sums[color], axis, offset, names[color]).astype(half)
                for offset in (1, -1, 2)
            ]
            going.append(pieces)
            arrived.append([shift(v, axis, n) for v, n in zip(pieces, (1, -1, 2))])
        sums, _ = lax.optimization_barrier((sums, going))
        for color in range(3):
            axis = ORDERS[color][stage]
            total = chunk(sums[color], axis, 0, names[color])
            for piece in arrived[color]:
                total = total + piece.astype(jnp.float32)
            sums[color] = total
            names[color] = names[color].replace(axis, "")
    result = jnp.concatenate([v.astype(half) for v in sums], axis=1)
    return result.reshape(micro, local_rows, width)


def solution(mesh):
    fine = Mesh(mesh.devices.reshape(4, 4, 4, 2), ("x", "y", "z", "c"))
    row = P(None, ("x", "y", "z", "c"), None)
    column = P(("y", "z", "c"), None, "x")
    in_specs = (row, row, row, P(), column, column, P(("y", "z", "c"), "x", None))
    return jax.shard_map(body, mesh=fine, in_specs=in_specs, out_specs=row, check_vma=False)
```

```python
import functools

import jax
import jax.numpy as jnp
from jax import lax
from jax.experimental import pallas as pl
from jax.experimental.pallas import tpu as pltpu
from jax.sharding import Mesh, PartitionSpec as P


META = 128
TK = 1024
TOP = 8
GROUP = 8
CAP = 2
BLOCK = 256
SEATS = BLOCK // GROUP * CAP
ORDERS = (("z", "y", "x"), ("y", "x", "z"), ("x", "z", "y"))


def gate_up_kernel(
    local_ref, x_ref, meta_ref, wg_ref, wu_ref, pg_ref, pu_ref, h_ref, acc, packed, select, scale
):
    k = pl.program_id(0)
    rows, _ = x_ref.shape
    hid = wg_ref.shape[2]
    blocks = rows // BLOCK
    top = TOP

    @pl.when(k == 0)
    def _():
        acc[...] = jnp.zeros_like(acc)
        early = lax.broadcasted_iota(jnp.int32, (BLOCK, BLOCK), 0)
        late = lax.broadcasted_iota(jnp.int32, (BLOCK, BLOCK), 1)
        before = ((early < late) & (early // GROUP == late // GROUP)).astype(jnp.bfloat16)
        place = lax.broadcasted_iota(jnp.int32, (SEATS, BLOCK), 0).astype(jnp.float32)
        group = lax.broadcasted_iota(jnp.int32, (1, BLOCK), 1) // GROUP
        seat0 = (group * CAP).astype(jnp.float32)
        for b in range(blocks):
            info = meta_ref[b * BLOCK : (b + 1) * BLOCK, :].astype(jnp.float32).T
            chosen = info[:top]
            weight = info[top : 2 * top] + info[2 * top : 3 * top] + info[3 * top : 4 * top]
            for j in range(4):
                hit = chosen == local_ref[j]
                coef = jnp.sum(jnp.where(hit, weight, 0.0), axis=0, keepdims=True)
                active = jnp.sum(jnp.where(hit, 1.0, 0.0), axis=0, keepdims=True)
                earlier = jnp.dot(
                    jnp.broadcast_to(active, (8, BLOCK)).astype(jnp.bfloat16),
                    before,
                    preferred_element_type=jnp.float32,
                )[:1]
                seat = jnp.where(active > 0.5, seat0 + earlier, -1.0)
                taken = place == seat
                select[b, j * SEATS : (j + 1) * SEATS, :] = jnp.where(taken, 1.0, 0.0).astype(
                    jnp.bfloat16
                )
                picked = jnp.sum(jnp.where(taken, coef, 0.0), axis=1, keepdims=True)
                scale[j, b * SEATS : (b + 1) * SEATS, :] = jnp.broadcast_to(picked, (SEATS, 128))

    for b in range(blocks):
        got = jnp.dot(
            select[b], x_ref[b * BLOCK : (b + 1) * BLOCK, :], preferred_element_type=jnp.float32
        ).astype(jnp.bfloat16)
        for j in range(4):
            packed[j, b * SEATS : (b + 1) * SEATS, :] = got[j * SEATS : (j + 1) * SEATS]
    for j in range(4):
        gate_w, up_w = ((wg_ref, wu_ref), (pg_ref, pu_ref))[j // 2]
        x = packed[j]
        acc[j, 0] += jnp.dot(x, gate_w[j % 2], preferred_element_type=jnp.float32)
        acc[j, 1] += jnp.dot(x, up_w[j % 2], preferred_element_type=jnp.float32)

    @pl.when(k == pl.num_programs(0) - 1)
    def _():

        @pl.loop(0, 4)
        def _(j):
            value = jax.nn.silu(acc[j, 0]) * acc[j, 1] * scale[j, :, :1]
            value = value.astype(jnp.bfloat16)
            columns = pl.ds(pl.multiple_of(j * hid, hid), hid)
            seats = pl.ds(pl.multiple_of(j * SEATS, SEATS), SEATS)
            for b in range(blocks):
                spread = select[b, seats, :].astype(jnp.float32).T
                h_ref[b * BLOCK : (b + 1) * BLOCK, columns] = jnp.dot(
                    spread.astype(jnp.bfloat16),
                    value[b * SEATS : (b + 1) * SEATS],
                    preferred_element_type=jnp.float32,
                ).astype(jnp.bfloat16)


def gate_up(local, x, wg, wu, pg, pu):
    rows = x.shape[0]
    depth, hid = wg.shape[1], wg.shape[2]
    packed_rows = rows // BLOCK * SEATS
    wspec = pl.BlockSpec((2, TK, hid), lambda k: (0, k, 0))
    return pl.pallas_call(
        gate_up_kernel,
        grid=(depth // TK,),
        in_specs=[
            pl.BlockSpec(memory_space=pltpu.SMEM),
            pl.BlockSpec((rows, TK), lambda k: (0, k)),
            pl.BlockSpec((rows, META), lambda k: (0, depth // META)),
            wspec,
            wspec,
            wspec,
            wspec,
        ],
        out_specs=pl.BlockSpec((rows, 4 * hid), lambda k: (0, 0)),
        out_shape=jax.ShapeDtypeStruct((rows, 4 * hid), jnp.bfloat16),
        scratch_shapes=[
            pltpu.VMEM((4, 2, packed_rows, hid), jnp.float32),
            pltpu.VMEM((4, packed_rows, TK), jnp.bfloat16),
            pltpu.VMEM((rows // BLOCK, 4 * SEATS, BLOCK), jnp.bfloat16),
            pltpu.VMEM((4, packed_rows, 128), jnp.float32),
        ],
        compiler_params=pltpu.CompilerParams(
            dimension_semantics=("arbitrary",), vmem_limit_bytes=58 * 1024 * 1024
        ),
        cost_estimate=pl.CostEstimate(
            flops=2 * packed_rows * depth * 8 * hid,
            bytes_accessed=2 * (rows * depth + 8 * depth * hid),
            transcendentals=packed_rows * 4 * hid,
        ),
    )(local, x, x, wg, wu, pg, pu)


def join_kernel(own_ref, other_ref, out_ref):
    rows = own_ref.shape[0]
    out_ref[:rows] = own_ref[...]
    out_ref[rows:] = other_ref[...]


def join(own, other, lower, upper):
    rows = own.shape[0]
    first = lower // 128
    source = pl.BlockSpec((rows, 128), lambda n: (0, first + n))
    return pl.pallas_call(
        join_kernel,
        grid=((upper - lower) // 128,),
        in_specs=[source, source],
        out_specs=pl.BlockSpec((2 * rows, 128), lambda n: (0, n)),
        out_shape=jax.ShapeDtypeStruct((2 * rows, upper - lower), own.dtype),
        cost_estimate=pl.CostEstimate(
            flops=0, bytes_accessed=8 * rows * (upper - lower), transcendentals=0
        ),
    )(own, other)


def project_kernel(dim, picks, at_ref, h_ref, w_ref, *refs):
    outs, rows_ref = refs[:-1], refs[-1]
    lead = h_ref.shape[0] // 2

    @pl.when(pl.program_id(0) == 0)
    def _():
        start = 0
        for pair in picks:
            for side, pick in enumerate(pair):
                at = at_ref[pick]
                lo = side * lead
                if dim == 0:
                    part = h_ref[at, lo : lo + lead]
                elif dim == 1:
                    part = h_ref[lo : lo + lead, at]
                else:
                    part = h_ref[lo : lo + lead, :, at]
                part = part.reshape(-1, h_ref.shape[-1])
                rows_ref[start : start + part.shape[0]] = part
                start += part.shape[0]

    count = rows_ref.shape[0] // len(outs)
    for n, out in enumerate(outs):
        value = jnp.dot(
            rows_ref[n * count : (n + 1) * count], w_ref[...], preferred_element_type=jnp.float32
        )
        out[...] = value.astype(out.dtype).reshape(out.shape)


def project_late(grid, weights, at, dim, picks, dtype):
    size, depth = grid.shape[0], grid.shape[-1]
    rest = [n for i, n in enumerate(grid.shape[:3]) if i != dim] + [grid.shape[3]]
    columns = weights.shape[1]
    rows = rest[0] * rest[1] * rest[2]
    tile = columns // 3 if columns % 384 == 0 else columns // 4
    return pl.pallas_call(
        functools.partial(project_kernel, dim, picks),
        grid=(columns // tile,),
        in_specs=[
            pl.BlockSpec(memory_space=pltpu.SMEM),
            pl.BlockSpec(grid.shape, lambda n: (0, 0, 0, 0, 0)),
            pl.BlockSpec((depth, tile), lambda n: (0, n)),
        ],
        out_specs=[pl.BlockSpec((*rest, tile), lambda n: (0, 0, 0, n))] * len(picks),
        out_shape=[jax.ShapeDtypeStruct((*rest, columns), dtype)] * len(picks),
        scratch_shapes=[pltpu.VMEM((rows * len(picks), depth), jnp.bfloat16)],
        compiler_params=pltpu.CompilerParams(
            dimension_semantics=("arbitrary",), vmem_limit_bytes=60 * 1024 * 1024
        ),
        cost_estimate=pl.CostEstimate(
            flops=2 * rows * len(picks) * depth * columns,
            bytes_accessed=2 * depth * columns,
            transcendentals=0,
        ),
    )(at, grid, weights)


def shift(value, axis, by):
    size = lax.axis_size(axis)
    return lax.ppermute(value, axis, [(i, (i + by) % size) for i in range(size)])


def split_weights(w):
    hi = lax.reduce_precision(w, 8, 7)
    mid = lax.reduce_precision(w - hi, 8, 7)
    lo = lax.reduce_precision(w - hi - mid, 8, 7)
    return [v.astype(jnp.bfloat16) for v in (hi, mid, lo)]


def body(tokens, routes, route_weights, slot_expert, w_gate, w_up, w_down):
    micro, local_rows, width = tokens.shape
    slots = slot_expert.shape[0]
    per_device = w_gate.shape[0]
    core = lax.axis_index("c")
    sizes = {a: lax.axis_size(a) for a in "xyz"}
    half = jnp.bfloat16

    swap = [(0, 1), (1, 0)]
    p_gate = lax.ppermute(w_gate, "c", swap)
    p_up = lax.ppermute(w_up, "c", swap)
    p_down = lax.ppermute(w_down, "c", swap)

    meta = [routes.astype(half)] + split_weights(route_weights)
    pad = jnp.zeros((micro, local_rows, META - 4 * TOP), half)
    sent = jnp.concatenate([tokens] + meta + [pad], axis=2)
    sent = sent.reshape(micro * local_rows, width + META)
    gathered = lax.all_gather(sent, ("x", "y", "z"), axis=0, tiled=True)

    slot_ids = jnp.arange(slots, dtype=jnp.int32)
    same = slot_expert[:, None] == slot_expert[None, :]
    primary = ~jnp.any(same & (slot_ids[None, :] < slot_ids[:, None]), axis=1)
    held = jnp.where(primary, slot_expert, -1)
    chip = (lax.axis_index("y") * sizes["z"] + lax.axis_index("z")) * 2
    mine = lax.dynamic_slice(held, ((chip + core) * per_device,), (per_device,))
    theirs = lax.dynamic_slice(held, ((chip + 1 - core) * per_device,), (per_device,))
    local = jnp.concatenate([mine, theirs]).astype(jnp.float32)

    down_rows = per_device * w_down.shape[1]
    wide = width // (3 * BLOCK) * BLOCK
    cuts = [0, wide, 2 * wide, width]
    flat_own, flat_other = w_down.reshape(down_rows, width), p_down.reshape(down_rows, width)
    downs = [join(flat_own, flat_other, cuts[c], cuts[c + 1]) for c in range(3)]
    gathered, downs, local = lax.optimization_barrier((gathered, downs, local))

    hidden = gate_up(local, gathered, w_gate, w_up, p_gate, p_up)
    grid = hidden.reshape(
        sizes["x"], sizes["y"], sizes["z"], micro * local_rows, hidden.shape[1]
    )

    def chunk(array, axis, offset, names):
        at = lax.rem(lax.axis_index(axis) + offset + sizes[axis], sizes[axis])
        return lax.dynamic_index_in_dim(array, at, names.index(axis), keepdims=False)

    def project(color, parts):
        part = jnp.concatenate(parts)
        value = jnp.dot(
            part.reshape(-1, part.shape[-1]), downs[color], preferred_element_type=jnp.float32
        )
        return value.reshape(part.shape[:-1] + (value.shape[-1],))

    first = [order[0] for order in ORDERS]
    mid = grid.shape[0] // 2
    got = []
    for color, axis in enumerate(first):
        far = chunk(grid, axis, 2, "xyz")
        up = project(color, [far[:mid], chunk(grid, axis, 1, "xyz")[mid:]]).astype(half)
        down = project(color, [chunk(grid, axis, -1, "xyz")[:mid], far[mid:]]).astype(half)
        got.append((shift(up, axis, 1), shift(down, axis, -1)))
        grid, _, _ = lax.optimization_barrier((grid, up, down))
    kept = []
    for color, axis in enumerate(first):
        if color < 2:
            near = [chunk(grid, axis, 1, "xyz")[:mid], chunk(grid, axis, -1, "xyz")[mid:]]
            value = project(color, near + [chunk(grid, axis, 0, "xyz")])
            kept.append((value[: 2 * mid], value[2 * mid :]))
            continue
        place = lax.axis_index(axis) + sizes[axis]
        where = jnp.stack([lax.rem(place + n, sizes[axis]) for n in (0, 1, -1)])
        kept.append(
            project_late(
                grid, downs[color], where, "xyz".index(axis), ((1, 2), (0, 0)), jnp.float32
            )
        )
    last = []
    for color, axis in enumerate(first):
        near, _ = kept[color]
        up, down = got[color]
        near_up = (near[:mid] + up[:mid].astype(jnp.float32)).astype(half)
        near_down = (near[mid:] + down[mid:].astype(jnp.float32)).astype(half)
        near_up, near_down = lax.optimization_barrier((near_up, near_down))
        last.append((shift(near_up, axis, 1), shift(near_down, axis, -1)))
    sums = []
    for color, axis in enumerate(first):
        _, own = kept[color]
        up, down = [v.astype(jnp.float32) for v in got[color]]
        up2, down2 = [v.astype(jnp.float32) for v in last[color]]
        sums.append(
            jnp.concatenate([own[:mid] + up2 + down[:mid], own[mid:] + up[mid:] + down2])
        )
    names = ["xyz".replace(axis, "") for axis in first]
    for stage in (1, 2):
        going, arrived = [], []
        for color in range(3):
            axis = ORDERS[color][stage]
            pieces = [
                chunk(sums[color], axis, offset, names[color]).astype(half)
                for offset in (1, -1, 2)
            ]
            going.append(pieces)
            arrived.append([shift(v, axis, n) for v, n in zip(pieces, (1, -1, 2))])
        sums, _ = lax.optimization_barrier((sums, going))
        for color in range(3):
            axis = ORDERS[color][stage]
            total = chunk(sums[color], axis, 0, names[color])
            for piece in arrived[color]:
                total = total + piece.astype(jnp.float32)
            sums[color] = total
            names[color] = names[color].replace(axis, "")
    result = jnp.concatenate([v.astype(half) for v in sums], axis=1)
    return result.reshape(micro, local_rows, width)


def solution(mesh):
    fine = Mesh(mesh.devices.reshape(4, 4, 4, 2), ("x", "y", "z", "c"))
    row = P(None, ("x", "y", "z", "c"), None)
    column = P(("y", "z", "c"), None, "x")
    in_specs = (row, row, row, P(), column, column, P(("y", "z", "c"), "x", None))
    return jax.shard_map(body, mesh=fine, in_specs=in_specs, out_specs=row, check_vma=False)
```

```python
import functools

import jax
import jax.numpy as jnp
from jax import lax
from jax.experimental import pallas as pl
from jax.experimental.pallas import tpu as pltpu
from jax.sharding import Mesh, PartitionSpec as P


META = 128
TK = 1024
TOP = 8
GROUP = 8
CAP = 2
BLOCK = 256
SEATS = BLOCK // GROUP * CAP
ORDERS = (("z", "y", "x"), ("y", "x", "z"), ("x", "z", "y"))


def gate_up_kernel(
    local_ref, x_ref, meta_ref, wg_ref, wu_ref, pg_ref, pu_ref, h_ref, acc, packed, select, scale
):
    k = pl.program_id(0)
    rows, _ = x_ref.shape
    hid = wg_ref.shape[2]
    blocks = rows // BLOCK
    top = TOP

    @pl.when(k == 0)
    def _():
        acc[...] = jnp.zeros_like(acc)
        early = lax.broadcasted_iota(jnp.int32, (BLOCK, BLOCK), 0)
        late = lax.broadcasted_iota(jnp.int32, (BLOCK, BLOCK), 1)
        before = ((early < late) & (early // GROUP == late // GROUP)).astype(jnp.bfloat16)
        place = lax.broadcasted_iota(jnp.int32, (SEATS, BLOCK), 0).astype(jnp.float32)
        group = lax.broadcasted_iota(jnp.int32, (1, BLOCK), 1) // GROUP
        seat0 = (group * CAP).astype(jnp.float32)
        for b in range(blocks):
            info = meta_ref[b * BLOCK : (b + 1) * BLOCK, :].astype(jnp.float32).T
            chosen = info[:top]
            weight = info[top : 2 * top] + info[2 * top : 3 * top] + info[3 * top : 4 * top]
            for j in range(4):
                hit = chosen == local_ref[j]
                coef = jnp.sum(jnp.where(hit, weight, 0.0), axis=0, keepdims=True)
                active = jnp.sum(jnp.where(hit, 1.0, 0.0), axis=0, keepdims=True)
                earlier = jnp.dot(
                    jnp.broadcast_to(active, (8, BLOCK)).astype(jnp.bfloat16),
                    before,
                    preferred_element_type=jnp.float32,
                )[:1]
                seat = jnp.where(active > 0.5, seat0 + earlier, -1.0)
                taken = place == seat
                select[b, j * SEATS : (j + 1) * SEATS, :] = jnp.where(taken, 1.0, 0.0).astype(
                    jnp.bfloat16
                )
                picked = jnp.sum(jnp.where(taken, coef, 0.0), axis=1, keepdims=True)
                scale[j, b * SEATS : (b + 1) * SEATS, :] = jnp.broadcast_to(picked, (SEATS, 128))

    for b in range(blocks):
        got = jnp.dot(
            select[b], x_ref[b * BLOCK : (b + 1) * BLOCK, :], preferred_element_type=jnp.float32
        ).astype(jnp.bfloat16)
        for j in range(4):
            packed[j, b * SEATS : (b + 1) * SEATS, :] = got[j * SEATS : (j + 1) * SEATS]
    for j in range(4):
        gate_w, up_w = ((wg_ref, wu_ref), (pg_ref, pu_ref))[j // 2]
        x = packed[j]
        acc[j, 0] += jnp.dot(x, gate_w[j % 2], preferred_element_type=jnp.float32)
        acc[j, 1] += jnp.dot(x, up_w[j % 2], preferred_element_type=jnp.float32)

    @pl.when(k == pl.num_programs(0) - 1)
    def _():

        @pl.loop(0, 4)
        def _(j):
            value = jax.nn.silu(acc[j, 0]) * acc[j, 1] * scale[j, :, :1]
            value = value.astype(jnp.bfloat16)
            columns = pl.ds(pl.multiple_of(j * hid, hid), hid)
            seats = pl.ds(pl.multiple_of(j * SEATS, SEATS), SEATS)
            for b in range(blocks):
                spread = select[b, seats, :].astype(jnp.float32).T
                h_ref[b * BLOCK : (b + 1) * BLOCK, columns] = jnp.dot(
                    spread.astype(jnp.bfloat16),
                    value[b * SEATS : (b + 1) * SEATS],
                    preferred_element_type=jnp.float32,
                ).astype(jnp.bfloat16)


def gate_up(local, x, wg, wu, pg, pu):
    rows = x.shape[0]
    depth, hid = wg.shape[1], wg.shape[2]
    packed_rows = rows // BLOCK * SEATS
    wspec = pl.BlockSpec((2, TK, hid), lambda k: (0, k, 0))
    return pl.pallas_call(
        gate_up_kernel,
        grid=(depth // TK,),
        in_specs=[
            pl.BlockSpec(memory_space=pltpu.SMEM),
            pl.BlockSpec((rows, TK), lambda k: (0, k)),
            pl.BlockSpec((rows, META), lambda k: (0, depth // META)),
            wspec,
            wspec,
            wspec,
            wspec,
        ],
        out_specs=pl.BlockSpec((rows, 4 * hid), lambda k: (0, 0)),
        out_shape=jax.ShapeDtypeStruct((rows, 4 * hid), jnp.bfloat16),
        scratch_shapes=[
            pltpu.VMEM((4, 2, packed_rows, hid), jnp.float32),
            pltpu.VMEM((4, packed_rows, TK), jnp.bfloat16),
            pltpu.VMEM((rows // BLOCK, 4 * SEATS, BLOCK), jnp.bfloat16),
            pltpu.VMEM((4, packed_rows, 128), jnp.float32),
        ],
        compiler_params=pltpu.CompilerParams(
            dimension_semantics=("arbitrary",), vmem_limit_bytes=58 * 1024 * 1024
        ),
        cost_estimate=pl.CostEstimate(
            flops=2 * packed_rows * depth * 8 * hid,
            bytes_accessed=2 * (rows * depth + 8 * depth * hid),
            transcendentals=packed_rows * 4 * hid,
        ),
    )(local, x, x, wg, wu, pg, pu)


def join_kernel(own_ref, other_ref, out_ref):
    rows = own_ref.shape[0]
    out_ref[:rows] = own_ref[...]
    out_ref[rows:] = other_ref[...]


def join(own, other, lower, upper):
    rows = own.shape[0]
    first = lower // 128
    source = pl.BlockSpec((rows, 128), lambda n: (0, first + n))
    return pl.pallas_call(
        join_kernel,
        grid=((upper - lower) // 128,),
        in_specs=[source, source],
        out_specs=pl.BlockSpec((2 * rows, 128), lambda n: (0, n)),
        out_shape=jax.ShapeDtypeStruct((2 * rows, upper - lower), own.dtype),
        cost_estimate=pl.CostEstimate(
            flops=0, bytes_accessed=8 * rows * (upper - lower), transcendentals=0
        ),
    )(own, other)


def project_kernel(dim, picks, at_ref, h_ref, w_ref, *refs):
    outs, rows_ref = refs[:-1], refs[-1]
    lead = h_ref.shape[0] // 2

    @pl.when(pl.program_id(0) == 0)
    def _():
        start = 0
        for pair in picks:
            for side, pick in enumerate(pair):
                at = at_ref[pick]
                lo = side * lead
                if dim == 0:
                    part = h_ref[at, lo : lo + lead]
                elif dim == 1:
                    part = h_ref[lo : lo + lead, at]
                else:
                    part = h_ref[lo : lo + lead, :, at]
                part = part.reshape(-1, h_ref.shape[-1])
                rows_ref[start : start + part.shape[0]] = part
                start += part.shape[0]

    count = rows_ref.shape[0] // len(outs)
    for n, out in enumerate(outs):
        value = jnp.dot(
            rows_ref[n * count : (n + 1) * count], w_ref[...], preferred_element_type=jnp.float32
        )
        out[...] = value.astype(out.dtype).reshape(out.shape)


def project_late(grid, weights, at, dim, picks, dtype):
    size, depth = grid.shape[0], grid.shape[-1]
    rest = [n for i, n in enumerate(grid.shape[:3]) if i != dim] + [grid.shape[3]]
    columns = weights.shape[1]
    rows = rest[0] * rest[1] * rest[2]
    tile = columns // 3 if columns % 384 == 0 else columns // 4
    return pl.pallas_call(
        functools.partial(project_kernel, dim, picks),
        grid=(columns // tile,),
        in_specs=[
            pl.BlockSpec(memory_space=pltpu.SMEM),
            pl.BlockSpec(grid.shape, lambda n: (0, 0, 0, 0, 0)),
            pl.BlockSpec((depth, tile), lambda n: (0, n)),
        ],
        out_specs=[pl.BlockSpec((*rest, tile), lambda n: (0, 0, 0, n))] * len(picks),
        out_shape=[jax.ShapeDtypeStruct((*rest, columns), dtype)] * len(picks),
        scratch_shapes=[pltpu.VMEM((rows * len(picks), depth), jnp.bfloat16)],
        compiler_params=pltpu.CompilerParams(
            dimension_semantics=("arbitrary",), vmem_limit_bytes=16 * 1024 * 1024
        ),
        cost_estimate=pl.CostEstimate(
            flops=2 * rows * len(picks) * depth * columns,
            bytes_accessed=2 * depth * columns,
            transcendentals=0,
        ),
    )(at, grid, weights)


def shift(value, axis, by):
    size = lax.axis_size(axis)
    return lax.ppermute(value, axis, [(i, (i + by) % size) for i in range(size)])


def split_weights(w):
    hi = lax.reduce_precision(w, 8, 7)
    mid = lax.reduce_precision(w - hi, 8, 7)
    lo = lax.reduce_precision(w - hi - mid, 8, 7)
    return [v.astype(jnp.bfloat16) for v in (hi, mid, lo)]


def body(tokens, routes, route_weights, slot_expert, w_gate, w_up, w_down):
    micro, local_rows, width = tokens.shape
    slots = slot_expert.shape[0]
    per_device = w_gate.shape[0]
    core = lax.axis_index("c")
    sizes = {a: lax.axis_size(a) for a in "xyz"}
    half = jnp.bfloat16

    swap = [(0, 1), (1, 0)]
    p_gate = lax.ppermute(w_gate, "c", swap)
    p_up = lax.ppermute(w_up, "c", swap)
    p_down = lax.ppermute(w_down, "c", swap)

    meta = [routes.astype(half)] + split_weights(route_weights)
    pad = jnp.zeros((micro, local_rows, META - 4 * TOP), half)
    sent = jnp.concatenate([tokens] + meta + [pad], axis=2)
    sent = sent.reshape(micro * local_rows, width + META)
    gathered = lax.all_gather(sent, ("x", "y", "z"), axis=0, tiled=True)

    slot_ids = jnp.arange(slots, dtype=jnp.int32)
    same = slot_expert[:, None] == slot_expert[None, :]
    primary = ~jnp.any(same & (slot_ids[None, :] < slot_ids[:, None]), axis=1)
    held = jnp.where(primary, slot_expert, -1)
    chip = (lax.axis_index("y") * sizes["z"] + lax.axis_index("z")) * 2
    mine = lax.dynamic_slice(held, ((chip + core) * per_device,), (per_device,))
    theirs = lax.dynamic_slice(held, ((chip + 1 - core) * per_device,), (per_device,))
    local = jnp.concatenate([mine, theirs]).astype(jnp.float32)

    down_rows = per_device * w_down.shape[1]
    wide = width // (3 * BLOCK) * BLOCK
    cuts = [0, wide, 2 * wide, width]
    flat_own, flat_other = w_down.reshape(down_rows, width), p_down.reshape(down_rows, width)
    downs = [join(flat_own, flat_other, cuts[c], cuts[c + 1]) for c in range(3)]
    gathered, downs, local = lax.optimization_barrier((gathered, downs, local))

    hidden = gate_up(local, gathered, w_gate, w_up, p_gate, p_up)
    grid = hidden.reshape(
        sizes["x"], sizes["y"], sizes["z"], micro * local_rows, hidden.shape[1]
    )

    def chunk(array, axis, offset, names):
        at = lax.rem(lax.axis_index(axis) + offset + sizes[axis], sizes[axis])
        return lax.dynamic_index_in_dim(array, at, names.index(axis), keepdims=False)

    def project(color, parts):
        part = jnp.concatenate(parts)
        value = jnp.dot(
            part.reshape(-1, part.shape[-1]), downs[color], preferred_element_type=jnp.float32
        )
        return value.reshape(part.shape[:-1] + (value.shape[-1],))

    first = [order[0] for order in ORDERS]
    mid = grid.shape[0] // 2
    got = []
    for color, axis in enumerate(first):
        far = chunk(grid, axis, 2, "xyz")
        up = project(color, [far[:mid], chunk(grid, axis, 1, "xyz")[mid:]]).astype(half)
        down = project(color, [chunk(grid, axis, -1, "xyz")[:mid], far[mid:]]).astype(half)
        got.append((shift(up, axis, 1), shift(down, axis, -1)))
        grid, _, _ = lax.optimization_barrier((grid, up, down))
    kept = []
    for color, axis in enumerate(first):
        if color < 2:
            near = [chunk(grid, axis, 1, "xyz")[:mid], chunk(grid, axis, -1, "xyz")[mid:]]
            value = project(color, near + [chunk(grid, axis, 0, "xyz")])
            kept.append((value[: 2 * mid], value[2 * mid :]))
            continue
        place = lax.axis_index(axis) + sizes[axis]
        where = jnp.stack([lax.rem(place + n, sizes[axis]) for n in (0, 1, -1)])
        kept.append(
            project_late(
                grid, downs[color], where, "xyz".index(axis), ((1, 2), (0, 0)), jnp.float32
            )
        )
    last = []
    for color, axis in enumerate(first):
        near, _ = kept[color]
        up, down = got[color]
        near_up = (near[:mid] + up[:mid].astype(jnp.float32)).astype(half)
        near_down = (near[mid:] + down[mid:].astype(jnp.float32)).astype(half)
        near_up, near_down = lax.optimization_barrier((near_up, near_down))
        last.append((shift(near_up, axis, 1), shift(near_down, axis, -1)))
    sums = []
    for color, axis in enumerate(first):
        _, own = kept[color]
        up, down = [v.astype(jnp.float32) for v in got[color]]
        up2, down2 = [v.astype(jnp.float32) for v in last[color]]
        sums.append(
            jnp.concatenate([own[:mid] + up2 + down[:mid], own[mid:] + up[mid:] + down2])
        )
    names = ["xyz".replace(axis, "") for axis in first]
    for stage in (1, 2):
        going, arrived = [], []
        for color in range(3):
            axis = ORDERS[color][stage]
            pieces = [
                chunk(sums[color], axis, offset, names[color]).astype(half)
                for offset in (1, -1, 2)
            ]
            going.append(pieces)
            arrived.append([shift(v, axis, n) for v, n in zip(pieces, (1, -1, 2))])
        sums, _ = lax.optimization_barrier((sums, going))
        for color in range(3):
            axis = ORDERS[color][stage]
            total = chunk(sums[color], axis, 0, names[color])
            for piece in arrived[color]:
                total = total + piece.astype(jnp.float32)
            sums[color] = total
            names[color] = names[color].replace(axis, "")
    result = jnp.concatenate([v.astype(half) for v in sums], axis=1)
    return result.reshape(micro, local_rows, width)


def solution(mesh):
    fine = Mesh(mesh.devices.reshape(4, 4, 4, 2), ("x", "y", "z", "c"))
    row = P(None, ("x", "y", "z", "c"), None)
    column = P(("y", "z", "c"), None, "x")
    in_specs = (row, row, row, P(), column, column, P(("y", "z", "c"), "x", None))
    return jax.shard_map(body, mesh=fine, in_specs=in_specs, out_specs=row, check_vma=False)
```

```python
import functools

import jax
import jax.numpy as jnp
from jax import lax
from jax.experimental import pallas as pl
from jax.experimental.pallas import tpu as pltpu
from jax.sharding import Mesh, PartitionSpec as P


META = 128
TK = 1024
TOP = 8
GROUP = 8
CAP = 2
BLOCK = 256
SEATS = BLOCK // GROUP * CAP
ORDERS = (("z", "y", "x"), ("y", "x", "z"), ("x", "z", "y"))


def gate_up_kernel(
    local_ref, x_ref, meta_ref, wg_ref, wu_ref, pg_ref, pu_ref, h_ref, acc, packed, select, scale
):
    k = pl.program_id(0)
    rows, _ = x_ref.shape
    hid = wg_ref.shape[2]
    blocks = rows // BLOCK
    top = TOP

    @pl.when(k == 0)
    def _():
        acc[...] = jnp.zeros_like(acc)
        early = lax.broadcasted_iota(jnp.int32, (BLOCK, BLOCK), 0)
        late = lax.broadcasted_iota(jnp.int32, (BLOCK, BLOCK), 1)
        before = ((early < late) & (early // GROUP == late // GROUP)).astype(jnp.bfloat16)
        place = lax.broadcasted_iota(jnp.int32, (SEATS, BLOCK), 0).astype(jnp.float32)
        group = lax.broadcasted_iota(jnp.int32, (1, BLOCK), 1) // GROUP
        seat0 = (group * CAP).astype(jnp.float32)
        for b in range(blocks):
            info = meta_ref[b * BLOCK : (b + 1) * BLOCK, :].astype(jnp.float32).T
            chosen = info[:top]
            weight = info[top : 2 * top] + info[2 * top : 3 * top] + info[3 * top : 4 * top]
            for j in range(4):
                hit = chosen == local_ref[j]
                coef = jnp.sum(jnp.where(hit, weight, 0.0), axis=0, keepdims=True)
                active = jnp.sum(jnp.where(hit, 1.0, 0.0), axis=0, keepdims=True)
                earlier = jnp.dot(
                    jnp.broadcast_to(active, (8, BLOCK)).astype(jnp.bfloat16),
                    before,
                    preferred_element_type=jnp.float32,
                )[:1]
                seat = jnp.where(active > 0.5, seat0 + earlier, -1.0)
                taken = place == seat
                select[b, j * SEATS : (j + 1) * SEATS, :] = jnp.where(taken, 1.0, 0.0).astype(
                    jnp.bfloat16
                )
                picked = jnp.sum(jnp.where(taken, coef, 0.0), axis=1, keepdims=True)
                scale[j, b * SEATS : (b + 1) * SEATS, :] = jnp.broadcast_to(picked, (SEATS, 128))

    for b in range(blocks):
        got = jnp.dot(
            select[b], x_ref[b * BLOCK : (b + 1) * BLOCK, :], preferred_element_type=jnp.float32
        ).astype(jnp.bfloat16)
        for j in range(4):
            packed[j, b * SEATS : (b + 1) * SEATS, :] = got[j * SEATS : (j + 1) * SEATS]
    for j in range(4):
        gate_w, up_w = ((wg_ref, wu_ref), (pg_ref, pu_ref))[j // 2]
        x = packed[j]
        acc[j, 0] += jnp.dot(x, gate_w[j % 2], preferred_element_type=jnp.float32)
        acc[j, 1] += jnp.dot(x, up_w[j % 2], preferred_element_type=jnp.float32)

    @pl.when(k == pl.num_programs(0) - 1)
    def _():

        @pl.loop(0, 4)
        def _(j):
            value = jax.nn.silu(acc[j, 0]) * acc[j, 1] * scale[j, :, :1]
            value = value.astype(jnp.bfloat16)
            columns = pl.ds(pl.multiple_of(j * hid, hid), hid)
            seats = pl.ds(pl.multiple_of(j * SEATS, SEATS), SEATS)
            for b in range(blocks):
                spread = select[b, seats, :].astype(jnp.float32).T
                h_ref[b * BLOCK : (b + 1) * BLOCK, columns] = jnp.dot(
                    spread.astype(jnp.bfloat16),
                    value[b * SEATS : (b + 1) * SEATS],
                    preferred_element_type=jnp.float32,
                ).astype(jnp.bfloat16)


def gate_up(local, x, wg, wu, pg, pu):
    rows = x.shape[0]
    depth, hid = wg.shape[1], wg.shape[2]
    packed_rows = rows // BLOCK * SEATS
    wspec = pl.BlockSpec((2, TK, hid), lambda k: (0, k, 0))
    return pl.pallas_call(
        gate_up_kernel,
        grid=(depth // TK,),
        in_specs=[
            pl.BlockSpec(memory_space=pltpu.SMEM),
            pl.BlockSpec((rows, TK), lambda k: (0, k)),
            pl.BlockSpec((rows, META), lambda k: (0, depth // META)),
            wspec,
            wspec,
            wspec,
            wspec,
        ],
        out_specs=pl.BlockSpec((rows, 4 * hid), lambda k: (0, 0)),
        out_shape=jax.ShapeDtypeStruct((rows, 4 * hid), jnp.bfloat16),
        scratch_shapes=[
            pltpu.VMEM((4, 2, packed_rows, hid), jnp.float32),
            pltpu.VMEM((4, packed_rows, TK), jnp.bfloat16),
            pltpu.VMEM((rows // BLOCK, 4 * SEATS, BLOCK), jnp.bfloat16),
            pltpu.VMEM((4, packed_rows, 128), jnp.float32),
        ],
        compiler_params=pltpu.CompilerParams(
            dimension_semantics=("arbitrary",), vmem_limit_bytes=54 * 1024 * 1024
        ),
        cost_estimate=pl.CostEstimate(
            flops=2 * packed_rows * depth * 8 * hid,
            bytes_accessed=2 * (rows * depth + 8 * depth * hid),
            transcendentals=packed_rows * 4 * hid,
        ),
    )(local, x, x, wg, wu, pg, pu)


def join_kernel(own_ref, other_ref, out_ref):
    rows = own_ref.shape[0]
    out_ref[:rows] = own_ref[...]
    out_ref[rows:] = other_ref[...]


def join(own, other, lower, upper):
    rows = own.shape[0]
    first = lower // 128
    source = pl.BlockSpec((rows, 128), lambda n: (0, first + n))
    return pl.pallas_call(
        join_kernel,
        grid=((upper - lower) // 128,),
        in_specs=[source, source],
        out_specs=pl.BlockSpec((2 * rows, 128), lambda n: (0, n)),
        out_shape=jax.ShapeDtypeStruct((2 * rows, upper - lower), own.dtype),
        cost_estimate=pl.CostEstimate(
            flops=0, bytes_accessed=8 * rows * (upper - lower), transcendentals=0
        ),
    )(own, other)


def project_kernel(dim, picks, at_ref, h_ref, w_ref, *refs):
    outs, rows_ref = refs[:-1], refs[-1]
    lead = h_ref.shape[0] // 2

    @pl.when(pl.program_id(0) == 0)
    def _():
        start = 0
        for pair in picks:
            for side, pick in enumerate(pair):
                at = at_ref[pick]
                lo = side * lead
                if dim == 0:
                    part = h_ref[at, lo : lo + lead]
                elif dim == 1:
                    part = h_ref[lo : lo + lead, at]
                else:
                    part = h_ref[lo : lo + lead, :, at]
                part = part.reshape(-1, h_ref.shape[-1])
                rows_ref[start : start + part.shape[0]] = part
                start += part.shape[0]

    count = rows_ref.shape[0] // len(outs)
    for n, out in enumerate(outs):
        value = jnp.dot(
            rows_ref[n * count : (n + 1) * count], w_ref[...], preferred_element_type=jnp.float32
        )
        out[...] = value.astype(out.dtype).reshape(out.shape)


def project_late(grid, weights, at, dim, picks, dtype):
    size, depth = grid.shape[0], grid.shape[-1]
    rest = [n for i, n in enumerate(grid.shape[:3]) if i != dim] + [grid.shape[3]]
    columns = weights.shape[1]
    rows = rest[0] * rest[1] * rest[2]
    tile = columns // 3 if columns % 384 == 0 else columns // 4
    return pl.pallas_call(
        functools.partial(project_kernel, dim, picks),
        grid=(columns // tile,),
        in_specs=[
            pl.BlockSpec(memory_space=pltpu.SMEM),
            pl.BlockSpec(grid.shape, lambda n: (0, 0, 0, 0, 0)),
            pl.BlockSpec((depth, tile), lambda n: (0, n)),
        ],
        out_specs=[pl.BlockSpec((*rest, tile), lambda n: (0, 0, 0, n))] * len(picks),
        out_shape=[jax.ShapeDtypeStruct((*rest, columns), dtype)] * len(picks),
        scratch_shapes=[pltpu.VMEM((rows * len(picks), depth), jnp.bfloat16)],
        compiler_params=pltpu.CompilerParams(
            dimension_semantics=("arbitrary",), vmem_limit_bytes=16 * 1024 * 1024
        ),
        cost_estimate=pl.CostEstimate(
            flops=2 * rows * len(picks) * depth * columns,
            bytes_accessed=2 * depth * columns,
            transcendentals=0,
        ),
    )(at, grid, weights)


def shift(value, axis, by):
    size = lax.axis_size(axis)
    return lax.ppermute(value, axis, [(i, (i + by) % size) for i in range(size)])


def split_weights(w):
    hi = lax.reduce_precision(w, 8, 7)
    mid = lax.reduce_precision(w - hi, 8, 7)
    lo = lax.reduce_precision(w - hi - mid, 8, 7)
    return [v.astype(jnp.bfloat16) for v in (hi, mid, lo)]


def body(tokens, routes, route_weights, slot_expert, w_gate, w_up, w_down):
    micro, local_rows, width = tokens.shape
    slots = slot_expert.shape[0]
    per_device = w_gate.shape[0]
    core = lax.axis_index("c")
    sizes = {a: lax.axis_size(a) for a in "xyz"}
    half = jnp.bfloat16

    swap = [(0, 1), (1, 0)]
    p_gate = lax.ppermute(w_gate, "c", swap)
    p_up = lax.ppermute(w_up, "c", swap)
    p_down = lax.ppermute(w_down, "c", swap)

    meta = [routes.astype(half)] + split_weights(route_weights)
    pad = jnp.zeros((micro, local_rows, META - 4 * TOP), half)
    sent = jnp.concatenate([tokens] + meta + [pad], axis=2)
    sent = sent.reshape(micro * local_rows, width + META)
    gathered = lax.all_gather(sent, ("x", "y", "z"), axis=0, tiled=True)

    slot_ids = jnp.arange(slots, dtype=jnp.int32)
    same = slot_expert[:, None] == slot_expert[None, :]
    primary = ~jnp.any(same & (slot_ids[None, :] < slot_ids[:, None]), axis=1)
    held = jnp.where(primary, slot_expert, -1)
    chip = (lax.axis_index("y") * sizes["z"] + lax.axis_index("z")) * 2
    mine = lax.dynamic_slice(held, ((chip + core) * per_device,), (per_device,))
    theirs = lax.dynamic_slice(held, ((chip + 1 - core) * per_device,), (per_device,))
    local = jnp.concatenate([mine, theirs]).astype(jnp.float32)

    down_rows = per_device * w_down.shape[1]
    wide = width // (3 * BLOCK) * BLOCK
    cuts = [0, wide, 2 * wide, width]
    flat_own, flat_other = w_down.reshape(down_rows, width), p_down.reshape(down_rows, width)
    downs = [join(flat_own, flat_other, cuts[c], cuts[c + 1]) for c in range(3)]
    gathered, downs, local = lax.optimization_barrier((gathered, downs, local))

    hidden = gate_up(local, gathered, w_gate, w_up, p_gate, p_up)
    grid = hidden.reshape(
        sizes["x"], sizes["y"], sizes["z"], micro * local_rows, hidden.shape[1]
    )

    def chunk(array, axis, offset, names):
        at = lax.rem(lax.axis_index(axis) + offset + sizes[axis], sizes[axis])
        return lax.dynamic_index_in_dim(array, at, names.index(axis), keepdims=False)

    def project(color, parts):
        part = jnp.concatenate(parts)
        value = jnp.dot(
            part.reshape(-1, part.shape[-1]), downs[color], preferred_element_type=jnp.float32
        )
        return value.reshape(part.shape[:-1] + (value.shape[-1],))

    first = [order[0] for order in ORDERS]
    mid = grid.shape[0] // 2
    got = []
    for color, axis in enumerate(first):
        far = chunk(grid, axis, 2, "xyz")
        up = project(color, [far[:mid], chunk(grid, axis, 1, "xyz")[mid:]]).astype(half)
        down = project(color, [chunk(grid, axis, -1, "xyz")[:mid], far[mid:]]).astype(half)
        got.append((shift(up, axis, 1), shift(down, axis, -1)))
        grid, _, _ = lax.optimization_barrier((grid, up, down))
    kept = []
    for color, axis in enumerate(first):
        if color < 2:
            near = [chunk(grid, axis, 1, "xyz")[:mid], chunk(grid, axis, -1, "xyz")[mid:]]
            value = project(color, near + [chunk(grid, axis, 0, "xyz")])
            kept.append((value[: 2 * mid], value[2 * mid :]))
            continue
        place = lax.axis_index(axis) + sizes[axis]
        where = jnp.stack([lax.rem(place + n, sizes[axis]) for n in (0, 1, -1)])
        kept.append(
            project_late(
                grid, downs[color], where, "xyz".index(axis), ((1, 2), (0, 0)), jnp.float32
            )
        )
    last = []
    for color, axis in enumerate(first):
        near, _ = kept[color]
        up, down = got[color]
        near_up = (near[:mid] + up[:mid].astype(jnp.float32)).astype(half)
        near_down = (near[mid:] + down[mid:].astype(jnp.float32)).astype(half)
        near_up, near_down = lax.optimization_barrier((near_up, near_down))
        last.append((shift(near_up, axis, 1), shift(near_down, axis, -1)))
    sums = []
    for color, axis in enumerate(first):
        _, own = kept[color]
        up, down = [v.astype(jnp.float32) for v in got[color]]
        up2, down2 = [v.astype(jnp.float32) for v in last[color]]
        sums.append(
            jnp.concatenate([own[:mid] + up2 + down[:mid], own[mid:] + up[mid:] + down2])
        )
    names = ["xyz".replace(axis, "") for axis in first]
    for stage in (1, 2):
        going, arrived = [], []
        for color in range(3):
            axis = ORDERS[color][stage]
            pieces = [
                chunk(sums[color], axis, offset, names[color]).astype(half)
                for offset in (1, -1, 2)
            ]
            going.append(pieces)
            arrived.append([shift(v, axis, n) for v, n in zip(pieces, (1, -1, 2))])
        sums, _ = lax.optimization_barrier((sums, going))
        for color in range(3):
            axis = ORDERS[color][stage]
            total = chunk(sums[color], axis, 0, names[color])
            for piece in arrived[color]:
                total = total + piece.astype(jnp.float32)
            sums[color] = total
            names[color] = names[color].replace(axis, "")
    result = jnp.concatenate([v.astype(half) for v in sums], axis=1)
    return result.reshape(micro, local_rows, width)


def solution(mesh):
    fine = Mesh(mesh.devices.reshape(4, 4, 4, 2), ("x", "y", "z", "c"))
    row = P(None, ("x", "y", "z", "c"), None)
    column = P(("y", "z", "c"), None, "x")
    in_specs = (row, row, row, P(), column, column, P(("y", "z", "c"), "x", None))
    return jax.shard_map(body, mesh=fine, in_specs=in_specs, out_specs=row, check_vma=False)
```
